32 devices in a mesh: dom: 16 (over z, y, x), band: 2 (over core).
Axes of the slice: x: 2, y: 2, z: 4, core: 2. Of those that a mesh axis runs over, the one named last changes fastest.
Arguments:
- vectors: bfloat16 [8192, 768], P('dom', 'band'), may hold values from -16 to 16
- cell_ham: bfloat16 [8, 512, 512], replicated, may hold values from -0.25 to 0.25
- cell_type: int32 [32], P('dom'), may hold values from 0 to 7
- cell_nodes: int32 [32, 512], P('dom'), may hold values from 0 to 767, as said below
- shared_nodes: int32 [16, 256], P('dom'), may hold values from 0 to 511, as said below
Outputs:
- filtered: bfloat16 [8192, 768], P('dom', 'band')
- margin: float32 [2, 384, 768], P('band', 'dom')
The draws below stay inside these ranges and needn't reach their ends.
Inputs may be any that keep to these rules, and one draw needn't show every extreme that they name: `cell_nodes`: the 512 entries of each cell are distinct. `shared_nodes`: the 256 entries of each row are distinct.
All inputs are finite; a program needn't handle non-finite values.
Results may differ from the reference program's by a relative error of at most 0.0045.
Values may be sent and summed in bfloat16 or wider, within the bound.
A program may use at most 64 MiB of HBM per device.

```python
import jax
import jax.numpy as jnp
from jax import lax

CN = 512
BAND_DEV = 384
NTYPES = 8
GHOST = 128
NODES_DEV = 512
CELLS_DEV = 2
BANDS = 768
NODES = 8192
CELLS = 32
N_DOM = 16
N_BAND = 2


def pick_distinct(subkey, extent, chosen_count, leading_cell):
    scores = jax.random.permutation(subkey, extent).astype(jnp.int32)
    positions = jnp.arange(extent, dtype=jnp.int32)
    forced = jnp.where(leading_cell & (positions == 0), -2, jnp.where(leading_cell & (positions == extent - 1), -1, scores))
    ranked = jnp.argsort(forced, stable=True)
    picked = ranked[:chosen_count]
    return jax.random.permutation(jax.random.fold_in(subkey, 7), picked).astype(jnp.int32)


def draw_cell_nodes(key, part):
    extent = NODES_DEV + 2 * GHOST
    subkeys = jax.random.split(jax.random.fold_in(key, 11), CELLS)
    leading_cell = jnp.arange(CELLS) % CELLS_DEV == 0
    return jax.vmap(lambda subkey, leading: pick_distinct(subkey, extent, CN, leading))(subkeys, leading_cell).astype(jnp.int32)


def draw_shared_nodes(key, part):
    subkeys = jax.random.split(jax.random.fold_in(key, 13), N_DOM)
    leading_cell = jnp.ones((N_DOM,), dtype=bool)
    return jax.vmap(lambda subkey, leading: pick_distinct(subkey, NODES_DEV, 2 * GHOST, leading))(subkeys, leading_cell).astype(jnp.int32)


def draw_vectors(key, part):
    key_common, key_weight, key_noise = jax.random.split(jax.random.fold_in(key, 17), 3)
    key_pairing = jax.random.fold_in(key, 19)
    common = jax.random.normal(key_common, (NODES, 1), jnp.float32)
    weights = jax.random.normal(key_weight, (1, BANDS), jnp.float32)
    pairing = jax.random.permutation(key_pairing, N_DOM).astype(jnp.int32)
    node_domain = (jnp.arange(NODES, dtype=jnp.int32) // NODES_DEV).astype(jnp.int32)
    target_domain = pairing[node_domain]
    column_owner = (jnp.arange(BANDS, dtype=jnp.int32) % BAND_DEV // (BAND_DEV // N_DOM)).astype(jnp.int32)
    heavy = jnp.where(target_domain[:, None] == column_owner[None, :], 5.0, 1.0).astype(jnp.float32)
    noise = jax.random.normal(key_noise, (NODES, BANDS), jnp.float32)
    values = 0.7 * common * weights + 0.7 * noise
    return jnp.clip(values * heavy, -16.0, 16.0).astype(jnp.bfloat16)


def place_ends(drawn, key, low, high):
    spot = [jax.random.randint(jax.random.fold_in(key, axis), (), 0, length) for axis, length in enumerate(drawn.shape)]
    widest = drawn.shape.index(max(drawn.shape))
    next_to = spot[:widest] + [(spot[widest] + 1) % drawn.shape[widest]] + spot[widest + 1:]
    return drawn.at[tuple(spot)].set(low).at[tuple(next_to)].set(high)


def normal_values(stream_key, shape, scale, limit, kind=jnp.bfloat16):
    drawn = jax.random.normal(stream_key, shape, jnp.float32) * scale
    return jnp.minimum(jnp.maximum(drawn, -limit), limit).astype(kind)


def setup_inputs(seed: int = 0) -> dict:
    key_of = jax.random.split(jax.random.key(seed), 6)
    vectors = draw_vectors(jax.random.fold_in(key_of[5], 71), 0)
    cell_ham = normal_values(key_of[1], (NTYPES, CN, CN), CN ** -0.5, 0.25)
    cell_type = place_ends(jax.random.randint(key_of[2], (CELLS,), 0, NTYPES), jax.random.fold_in(key_of[2], 1), 0, NTYPES - 1).astype(jnp.int32)
    cell_nodes = draw_cell_nodes(jax.random.fold_in(key_of[5], 71), 0)
    shared_nodes = draw_shared_nodes(jax.random.fold_in(key_of[5], 71), 0)
    return dict(vectors=vectors, cell_ham=cell_ham, cell_type=cell_type, cell_nodes=cell_nodes, shared_nodes=shared_nodes)


SHIFT = 0.5
INV_HALF = 0.5


def extended_map(shared_nodes):
    domains = jnp.arange(N_DOM, dtype=jnp.int32)[:, None]
    absent = N_DOM * NODES_DEV
    preceding = jnp.roll(shared_nodes, 1, axis=0)[:, GHOST:]
    following = jnp.roll(shared_nodes, -1, axis=0)[:, :GHOST]
    lower_rim = jnp.where(domains > 0, (domains - 1) * NODES_DEV + preceding, absent)
    owned_rows = domains * NODES_DEV + jnp.arange(NODES_DEV, dtype=jnp.int32)[None, :]
    upper_rim = jnp.where(domains < N_DOM - 1, (domains + 1) * NODES_DEV + following, absent)
    return jnp.concatenate([lower_rim, owned_rows, upper_rim], axis=1).astype(jnp.int32)


def reference(vectors, cell_ham, cell_type, cell_nodes, shared_nodes):
    node_map = extended_map(shared_nodes)
    cell_domain = (jnp.arange(CELLS, dtype=jnp.int32) // CELLS_DEV).astype(jnp.int32)
    global_cells = node_map[cell_domain[:, None], cell_nodes].astype(jnp.int32)

    def apply_operator(field):
        padded = jnp.concatenate([field, jnp.zeros((1, field.shape[1]), field.dtype)], axis=0)

        def add_cell(accumulated, cell_item):
            node_index, cell_kind = cell_item
            cell_out = jnp.dot(cell_ham[cell_kind], padded[node_index], preferred_element_type=jnp.float32)
            return accumulated.at[node_index].add(cell_out), None

        initial = jnp.zeros((NODES + 1, BANDS), jnp.float32)
        accumulated, _ = lax.scan(add_cell, initial, (global_cells, cell_type))
        return accumulated[:-1]

    initial_f = vectors.astype(jnp.float32)
    first_section = ((apply_operator(vectors) - SHIFT * initial_f) * INV_HALF).astype(jnp.bfloat16)
    second = apply_operator(first_section)
    filtered = (2.0 * (second - SHIFT * first_section.astype(jnp.float32)) * INV_HALF - initial_f).astype(jnp.bfloat16)
    margin = jnp.dot(filtered.T, filtered, preferred_element_type=jnp.float32) * (1.0 / NODES)
    return filtered, margin.reshape(N_BAND, BAND_DEV, BANDS)
```

```python
import functools

import jax
import jax.numpy as jnp
from jax import lax
from jax.experimental import pallas as pl
from jax.experimental.pallas import tpu as pltpu
from jax.sharding import PartitionSpec as P

SHIFT = 0.5
INV_HALF = 0.5
GROUP = 4
WIDTHS = (128, 128, 128)
PIECES = ((0, 0, 384, 0), (1, 0, 128, 0), (1, 128, 384, 1))
ORDER = (0, 1, 2)
MESH = pl.DeviceIdType.MESH
F32 = jnp.float32
BF16 = jnp.bfloat16


def dot(a, b):
    return jnp.dot(a, b, preferred_element_type=F32)


def dot_tn(a, b):
    return lax.dot_general(a, b, (((0,), (0,)), ((), ())), preferred_element_type=F32)


def dot_nt(a, b):
    return lax.dot_general(a, b, (((1,), (1,)), ((), ())), preferred_element_type=F32)


def one_hot(rows, index_row):
    spots = lax.broadcasted_iota(jnp.int32, (rows, index_row.shape[1]), 0)
    return jnp.where(spots == index_row, 1.0, 0.0).astype(BF16)


def kernel(
    doms, bands, chunks, inverse_count,
    type_hbm, nodes_hbm, shared_hbm, v_hbm, ham_hbm,
    filt_ref, margin_ref,
    type_ref, nodes_ref, shared_ref, v_ref, ham, hp, hp_shared,
    send1, ghost, send2, recv2, send3, recv3, everyone,
    in_sem, s1, r1, s2, r2, s3, r3, s4, r4, known,
    *held_refs,
):
    dom = lax.axis_index("dom")
    band = lax.axis_index("band")
    nodes, cols = v_ref.shape
    cells = nodes_ref.shape[0]
    rim = shared_ref.shape[1] // 2
    slots = nodes + 2 * rim
    present = (dom > 0, dom < doms - 1)
    beside = (jnp.maximum(dom - 1, 0), jnp.minimum(dom + 1, doms - 1))

    load_shared, load_v, load_nodes, load_type, load_ham = [
        pltpu.make_async_copy(source, target, in_sem.at[number])
        for number, (source, target) in enumerate(
            (
                (shared_hbm, shared_ref),
                (v_hbm, v_ref),
                (nodes_hbm, nodes_ref),
                (type_hbm, type_ref),
                (ham_hbm, ham),
            )
        )
    ]

    barrier = pltpu.get_barrier_semaphore()

    def greet(other_dom, other_band):
        pl.semaphore_signal(
            barrier, inc=1,
            device_id={"dom": other_dom, "band": other_band},
            device_id_type=MESH,
        )

    for side in (0, 1):
        @pl.when(present[side])
        def _():
            greet(beside[side], band)
    for step in range(1, bands):
        greet(dom, lax.rem(band + step, bands))
    for load in (load_shared, load_v, load_nodes, load_type, load_ham):
        load.start()

    for side in (0, 1):
        @pl.when(jnp.logical_not(present[side]))
        def _():
            ghost[side] = jnp.zeros((rim, cols), BF16)
            recv2[side] = jnp.zeros((2, rim, cols), BF16)
            recv3[side] = jnp.zeros((rim, cols), BF16)

    def swap(source, target, sent, got, chunk, side, arriving):
        low, high = chunks[chunk]
        landing = side if arriving else 1 - side
        return pltpu.make_async_remote_copy(
            src_ref=source.at[side, ..., low:high],
            dst_ref=target.at[landing, ..., low:high],
            send_sem=sent.at[chunk, side],
            recv_sem=got.at[chunk, landing],
            device_id={"dom": beside[side], "band": band},
            device_id_type=MESH,
        )

    def swap_start(*args):
        for side in (0, 1):
            @pl.when(present[side])
            def _():
                swap(*args, side, False).start()

    def swap_wait(*args):
        for side in (0, 1):
            @pl.when(present[side])
            def _():
                swap(*args, side, True).wait()

    load_shared.wait()
    load_v.wait()
    pick = one_hot(nodes, shared_ref[...])
    send1[...] = dot_tn(pick, v_ref[...]).astype(BF16).reshape(2, rim, cols)

    pl.semaphore_wait(
        barrier,
        bands - 1 + jnp.where(present[0], 1, 0) + jnp.where(present[1], 1, 0),
    )
    numbers = range(len(chunks))
    for chunk in numbers:
        swap_start(send1, ghost, s1, r1, chunk)

    load_nodes.wait()
    load_type.wait()
    load_ham.wait()
    for cell in range(cells):
        slot = nodes_ref[cell : cell + 1, :]
        slot = jnp.where(slot < rim, slot + nodes, jnp.where(slot < nodes + rim, slot - rim, slot))
        spread = one_hot(slots, slot)
        spread_ham = dot(spread, ham[type_ref[cell]]).astype(BF16)
        hp[cell] = dot_nt(spread_ham, spread).astype(BF16)
        hp_shared[cell] = dot_tn(pick, hp[cell, :nodes, :]).astype(BF16)

    def apply(low, high, own, rims, matrix=hp):
        total = 0.0
        for cell in range(cells):
            total += dot(matrix[cell, low:high, :nodes], own)
            total += dot(matrix[cell, low:high, nodes:], rims)
        return total

    held = []
    for chunk, (low, high) in enumerate(chunks):
        wide = high - low
        swap_wait(send1, ghost, s1, r1, chunk)
        v = v_ref[:, low:high]
        rims = ghost[:, :, low:high].reshape(2 * rim, wide)
        y_rim = apply(nodes, slots, v, rims)
        send2[:, 0, :, low:high] = y_rim.astype(BF16).reshape(2, rim, wide)
        y_shared = apply(0, 2 * rim, v, rims, hp_shared)
        send2[:, 1, :, low:high] = y_shared.astype(BF16).reshape(2, rim, wide)
        swap_start(send2, recv2, s2, r2, chunk)
        y_own = apply(0, nodes, v, rims)
        held.append((y_own, y_rim))

    again = []
    for chunk, (low, high) in enumerate(chunks):
        wide = high - low
        y_own, y_rim = held[chunk]
        v32 = v_ref[:, low:high].astype(F32)
        rims = ghost[:, :, low:high].reshape(2 * rim, wide).astype(F32)
        swap_wait(send2, recv2, s2, r2, chunk)
        y_own = y_own + dot(pick, recv2[:, 0, :, low:high].reshape(2 * rim, wide))
        y_rim = y_rim + recv2[:, 1, :, low:high].reshape(2 * rim, wide).astype(F32)
        first = ((y_own - SHIFT * v32) * INV_HALF).astype(BF16)
        first_rim = ((y_rim - SHIFT * rims) * INV_HALF).reshape(2, rim, wide)
        first_rim = jnp.concatenate(
            [jnp.where(present[side], first_rim[side], 0.0) for side in (0, 1)], axis=0
        ).astype(BF16)
        out_rim = apply(nodes, slots, first, first_rim)
        send3[:, :, low:high] = out_rim.astype(BF16).reshape(2, rim, wide)
        swap_start(send3, recv3, s3, r3, chunk)
        again.append((apply(0, nodes, first, first_rim), first))

    inside, stack = lax.rem(dom, GROUP), dom // GROUP
    linked = (stack > 0, stack < doms // GROUP - 1)

    def announce(turn):
        if turn:
            hear(turn - 1)
        for side in (0, 1):
            @pl.when(linked[side])
            def _():
                pl.semaphore_signal(
                    known.at[turn, 1 - side], inc=1,
                    device_id={"dom": dom + (GROUP if side else -GROUP), "band": band},
                    device_id_type=MESH,
                )

    def hear(turn):
        for side in (0, 1):
            @pl.when(linked[side])
            def _():
                pl.semaphore_wait(known.at[turn, side], 1)

    def share(chunk, step, arriving=False):
        low, high = chunks[chunk]
        landing = step - 1 if arriving else bands - 1 - step
        return pltpu.make_async_remote_copy(
            src_ref=filt_ref.at[:, low:high],
            dst_ref=everyone.at[landing, :, low:high],
            send_sem=s4.at[chunk, step],
            recv_sem=r4.at[chunk, landing],
            device_id={"dom": dom, "band": lax.rem(band + step, bands)},
            device_id_type=MESH,
        )

    for chunk, (low, high) in enumerate(chunks):
        wide = high - low
        second, first = again[chunk]
        v32 = v_ref[:, low:high].astype(F32)
        swap_wait(send3, recv3, s3, r3, chunk)
        if chunk < 2:
            announce(chunk)
        second = second + dot(pick, recv3[:, :, low:high].reshape(2 * rim, wide))
        filt_ref[:, low:high] = (
            2.0 * (second - SHIFT * first.astype(F32)) * INV_HALF - v32
        ).astype(BF16)
        for step in range(1, bands):
            share(chunk, step).start()

    def place(step, low, high):
        start = lax.rem(band + step, bands) * cols + low
        return pl.ds(pl.multiple_of(start, 128), high - low)

    def others(step):
        if step == 0:
            return filt_ref[...]
        for chunk in numbers:
            share(chunk, step, True).wait_recv()
        return everyone[step - 1]

    rows = cols // doms
    where = (inside, stack)

    def device(axis, index):
        return stack * GROUP + index if axis == 0 else index * GROUP + inside

    def pass_on(axis, source, target, sent, got, away, arriving=False):
        other = lax.rem(where[axis] + away, GROUP)
        landing = away - 1 if arriving else GROUP - 1 - away
        return pltpu.make_async_remote_copy(
            src_ref=source.at[other],
            dst_ref=target.at[landing],
            send_sem=sent.at[away - 1],
            recv_sem=got.at[landing],
            device_id={"dom": device(axis, other), "band": band},
            device_id_type=MESH,
        )

    away_range = range(1, GROUP)
    works = [held_refs[number : number + 10] for number in range(0, len(held_refs), 10)]
    hear(1)
    for step in range(bands):
        product = dot_tn(filt_ref[...], others(step))
        for (its_step, low, high, axis), work in zip(PIECES, works):
            if its_step != step:
                continue
            part, own_part, arrived, s5, r5 = work[:5]
            for member in range(GROUP):
                if axis == 0:
                    block = jnp.concatenate(
                        [
                            product[(layer * GROUP + member) * rows : (layer * GROUP + member + 1) * rows, low:high]
                            for layer in range(GROUP)
                        ],
                        axis=0,
                    )
                else:
                    block = product[member * GROUP * rows : (member + 1) * GROUP * rows, low:high]
                own_part[member] = block
                part[member] = block.astype(BF16)
            for away in away_range:
                pass_on(axis, part, arrived, s5, r5, away).start()
    for number in ORDER:
        step, low, high, axis = PIECES[number]
        part, own_part, arrived, s5, r5, part2, own_part2, arrived2, s6, r6 = works[number]
        total = own_part[where[axis]]
        for away in away_range:
            pass_on(axis, part, arrived, s5, r5, away, True).wait_recv()
            total += arrived[away - 1].astype(F32)
        for layer in range(GROUP):
            block = total[layer * rows : (layer + 1) * rows]
            own_part2[layer] = block
            part2[layer] = block.astype(BF16)
        for away in away_range:
            pass_on(1 - axis, part2, arrived2, s6, r6, away).start()
    for number in ORDER:
        step, low, high, axis = PIECES[number]
        part, own_part, arrived, s5, r5, part2, own_part2, arrived2, s6, r6 = works[number]
        total = own_part2[where[1 - axis]]
        for away in away_range:
            pass_on(1 - axis, part2, arrived2, s6, r6, away, True).wait_recv()
            total += arrived2[away - 1].astype(F32)
        margin_ref[0, :, place(step, low, high)] = total * inverse_count
    for number, (step, low, high, axis) in enumerate(PIECES):
        part, own_part, arrived, s5, r5, part2, own_part2, arrived2, s6, r6 = works[number]
        for away in away_range:
            pass_on(axis, part, arrived, s5, r5, away).wait_send()
            pass_on(1 - axis, part2, arrived2, s6, r6, away).wait_send()
    for chunk in numbers:
        for step in range(1, bands):
            share(chunk, step).wait_send()


def plain_kernel(
    doms, bands, chunks,
    type_hbm, nodes_hbm, shared_hbm, v_hbm, ham_hbm,
    filt_ref, margin_ref,
    type_ref, nodes_ref, shared_ref, v_ref, ham, hp,
    send1, ghost, send2, recv2, send3, recv3, everyone,
    in_sem, s1, r1, s2, r2, s3, r3, s4, r4,
):
    dom = lax.axis_index("dom")
    band = lax.axis_index("band")
    nodes, cols = v_ref.shape
    cells = nodes_ref.shape[0]
    rim = shared_ref.shape[1] // 2
    slots = nodes + 2 * rim
    present = (dom > 0, dom < doms - 1)
    beside = (jnp.maximum(dom - 1, 0), jnp.minimum(dom + 1, doms - 1))

    load_shared, load_v, load_nodes, load_type, load_ham = [
        pltpu.make_async_copy(source, target, in_sem.at[number])
        for number, (source, target) in enumerate(
            (
                (shared_hbm, shared_ref),
                (v_hbm, v_ref),
                (nodes_hbm, nodes_ref),
                (type_hbm, type_ref),
                (ham_hbm, ham),
            )
        )
    ]

    barrier = pltpu.get_barrier_semaphore()

    def greet(other_dom, other_band):
        pl.semaphore_signal(
            barrier, inc=1,
            device_id={"dom": other_dom, "band": other_band},
            device_id_type=MESH,
        )

    for side in (0, 1):
        @pl.when(present[side])
        def _():
            greet(beside[side], band)
    for step in range(1, bands):
        greet(dom, lax.rem(band + step, bands))
    for load in (load_shared, load_v, load_nodes, load_type, load_ham):
        load.start()

    for side in (0, 1):
        @pl.when(jnp.logical_not(present[side]))
        def _():
            ghost[side] = jnp.zeros((rim, cols), BF16)
            recv2[side] = jnp.zeros((2, rim, cols), BF16)
            recv3[side] = jnp.zeros((rim, cols), BF16)

    def swap(source, target, sent, got, chunk, side, arriving):
        low, high = chunks[chunk]
        landing = side if arriving else 1 - side
        return pltpu.make_async_remote_copy(
            src_ref=source.at[side, ..., low:high],
            dst_ref=target.at[landing, ..., low:high],
            send_sem=sent.at[chunk, side],
            recv_sem=got.at[chunk, landing],
            device_id={"dom": beside[side], "band": band},
            device_id_type=MESH,
        )

    def swap_start(*args):
        for side in (0, 1):
            @pl.when(present[side])
            def _():
                swap(*args, side, False).start()

    def swap_wait(*args):
        for side in (0, 1):
            @pl.when(present[side])
            def _():
                swap(*args, side, True).wait()

    load_shared.wait()
    load_v.wait()
    pick = one_hot(nodes, shared_ref[...])
    send1[...] = dot_tn(pick, v_ref[...]).astype(BF16).reshape(2, rim, cols)

    pl.semaphore_wait(
        barrier,
        bands - 1 + jnp.where(present[0], 1, 0) + jnp.where(present[1], 1, 0),
    )
    numbers = range(len(chunks))
    for chunk in numbers:
        swap_start(send1, ghost, s1, r1, chunk)

    load_nodes.wait()
    load_type.wait()
    load_ham.wait()
    for cell in range(cells):
        slot = nodes_ref[cell : cell + 1, :]
        slot = jnp.where(slot < rim, slot + nodes, jnp.where(slot < nodes + rim, slot - rim, slot))
        spread = one_hot(slots, slot)
        spread_ham = dot(spread, ham[type_ref[cell]]).astype(BF16)
        hp[cell] = dot_nt(spread_ham, spread).astype(BF16)

    def apply(low, high, own, rims):
        total = dot(hp[0, low:high, :nodes], own) + dot(hp[0, low:high, nodes:], rims)
        for cell in range(1, cells):
            total += dot(hp[cell, low:high, :nodes], own) + dot(hp[cell, low:high, nodes:], rims)
        return total

    held = []
    for chunk, (low, high) in enumerate(chunks):
        wide = high - low
        swap_wait(send1, ghost, s1, r1, chunk)
        v = v_ref[:, low:high]
        rims = ghost[:, :, low:high].reshape(2 * rim, wide)
        y_own = apply(0, nodes, v, rims)
        send2[:, 1, :, low:high] = (
            dot_tn(pick, y_own.astype(BF16)).astype(BF16).reshape(2, rim, wide)
        )
        y_rim = apply(nodes, slots, v, rims)
        send2[:, 0, :, low:high] = y_rim.astype(BF16).reshape(2, rim, wide)
        swap_start(send2, recv2, s2, r2, chunk)
        held.append((y_own, y_rim))

    again = []
    for chunk, (low, high) in enumerate(chunks):
        wide = high - low
        y_own, y_rim = held[chunk]
        v32 = v_ref[:, low:high].astype(F32)
        rims = ghost[:, :, low:high].reshape(2 * rim, wide).astype(F32)
        swap_wait(send2, recv2, s2, r2, chunk)
        y_own = y_own + dot(pick, recv2[:, 0, :, low:high].reshape(2 * rim, wide))
        y_rim = y_rim + recv2[:, 1, :, low:high].reshape(2 * rim, wide).astype(F32)
        first = ((y_own - SHIFT * v32) * INV_HALF).astype(BF16)
        first_rim = ((y_rim - SHIFT * rims) * INV_HALF).reshape(2, rim, wide)
        first_rim = jnp.concatenate(
            [jnp.where(present[side], first_rim[side], 0.0) for side in (0, 1)], axis=0
        ).astype(BF16)
        out_rim = apply(nodes, slots, first, first_rim)
        send3[:, :, low:high] = out_rim.astype(BF16).reshape(2, rim, wide)
        swap_start(send3, recv3, s3, r3, chunk)
        again.append((apply(0, nodes, first, first_rim), first))

    def share(chunk, step, arriving=False):
        low, high = chunks[chunk]
        landing = step - 1 if arriving else bands - 1 - step
        return pltpu.make_async_remote_copy(
            src_ref=filt_ref.at[:, low:high],
            dst_ref=everyone.at[landing, :, low:high],
            send_sem=s4.at[chunk, step],
            recv_sem=r4.at[chunk, landing],
            device_id={"dom": dom, "band": lax.rem(band + step, bands)},
            device_id_type=MESH,
        )

    for chunk, (low, high) in enumerate(chunks):
        wide = high - low
        second, first = again[chunk]
        v32 = v_ref[:, low:high].astype(F32)
        swap_wait(send3, recv3, s3, r3, chunk)
        second = second + dot(pick, recv3[:, :, low:high].reshape(2 * rim, wide))
        filt_ref[:, low:high] = (
            2.0 * (second - SHIFT * first.astype(F32)) * INV_HALF - v32
        ).astype(BF16)
        for step in range(1, bands):
            share(chunk, step).start()

    def place(step):
        return pl.ds(pl.multiple_of(lax.rem(band + step, bands) * cols, 128), cols)

    for step in range(bands):
        if step == 0:
            other = filt_ref[...]
        else:
            for chunk in numbers:
                share(chunk, step, True).wait_recv()
            other = everyone[step - 1]
        product = dot_tn(filt_ref[...], other)
        margin_ref[0, :, place(step)] = product
    for chunk in numbers:
        for step in range(1, bands):
            share(chunk, step).wait_send()


def put_out(filt_ref, margin_ref, filt_hbm, margin_hbm, sem):
    copies = [
        pltpu.make_async_copy(source, target, sem.at[number])
        for number, (source, target) in enumerate(
            ((filt_ref, filt_hbm), (margin_ref, margin_hbm))
        )
    ]
    for copy in copies:
        copy.start()
    for copy in copies:
        copy.wait()


def solution(mesh):
    doms, bands = mesh.shape["dom"], mesh.shape["band"]

    def on_device(vectors, cell_ham, cell_type, cell_nodes, shared_nodes):
        nodes, cols = vectors.shape
        rim = shared_nodes.shape[1] // 2
        slots = nodes + 2 * rim
        rows = cols // doms
        scatter_here = cols % doms == 0 and rows % 8 == 0 and doms == GROUP * GROUP and bands == 2
        inverse_count = 1.0 / (nodes * doms)
        chunks = []
        for width in WIDTHS + (cols,):
            low = chunks[-1][1] if chunks else 0
            if low < cols:
                chunks.append((low, min(low + width, cols)))
        kept = []
        if scatter_here:
            for _, low, high, _ in PIECES:
                wide = high - low
                kept += [
                    pltpu.VMEM((GROUP, GROUP * rows, wide), BF16),
                    pltpu.VMEM((GROUP, GROUP * rows, wide), F32),
                    pltpu.VMEM((GROUP - 1, GROUP * rows, wide), BF16),
                ]
                kept += [pltpu.SemaphoreType.DMA((GROUP - 1,))] * 2
                kept += [
                    pltpu.VMEM((GROUP, rows, wide), BF16),
                    pltpu.VMEM((GROUP, rows, wide), F32),
                    pltpu.VMEM((GROUP - 1, rows, wide), BF16),
                ]
                kept += [pltpu.SemaphoreType.DMA((GROUP - 1,))] * 2
        operands = [
            pltpu.with_memory_space_constraint(operand, pltpu.HBM)
            for operand in (cell_type, cell_nodes, shared_nodes, vectors, cell_ham)
        ]
        if scatter_here:
            filtered, margin = pl.pallas_call(
                functools.partial(kernel, doms, bands, tuple(chunks), inverse_count),
                out_shape=(
                    jax.ShapeDtypeStruct((nodes, cols), BF16),
                    jax.ShapeDtypeStruct((1, rows, bands * cols), F32),
                ),
                in_specs=[pl.BlockSpec(memory_space=pltpu.HBM)] * 5,
                out_specs=(pl.BlockSpec(memory_space=pltpu.VMEM),) * 2,
                scratch_shapes=[
                    pltpu.SMEM(cell_type.shape, jnp.int32),
                    pltpu.VMEM(cell_nodes.shape, jnp.int32),
                    pltpu.VMEM(shared_nodes.shape, jnp.int32),
                    pltpu.VMEM(vectors.shape, BF16),
                    pltpu.VMEM(cell_ham.shape, BF16),
                    pltpu.VMEM((cell_nodes.shape[0], slots, slots), BF16),
                    pltpu.VMEM((cell_nodes.shape[0], 2 * rim, slots), BF16),
                    pltpu.VMEM((2, rim, cols), BF16),
                    pltpu.VMEM((2, rim, cols), BF16),
                    pltpu.VMEM((2, 2, rim, cols), BF16),
                    pltpu.VMEM((2, 2, rim, cols), BF16),
                    pltpu.VMEM((2, rim, cols), BF16),
                    pltpu.VMEM((2, rim, cols), BF16),
                    pltpu.VMEM((max(bands - 1, 1), nodes, cols), BF16),
                ]
                + [pltpu.SemaphoreType.DMA((5,))]
                + [pltpu.SemaphoreType.DMA((len(chunks), 2))] * 6
                + [pltpu.SemaphoreType.DMA((len(chunks), bands))] * 2
                + [pltpu.SemaphoreType.REGULAR((2, 2))]
                + kept,
                compiler_params=pltpu.CompilerParams(
                    collective_id=0, has_side_effects=True, vmem_limit_bytes=48 << 20
                ),
            )(*operands)
            filtered, margin = [
                pltpu.with_memory_space_constraint(result, pltpu.VMEM)
                for result in (filtered, margin)
            ]
            filtered, margin = pl.pallas_call(
                put_out,
                out_shape=(
                    jax.ShapeDtypeStruct(filtered.shape, BF16),
                    jax.ShapeDtypeStruct(margin.shape, F32),
                ),
                in_specs=[pl.BlockSpec(memory_space=pltpu.VMEM)] * 2,
                out_specs=(pl.BlockSpec(memory_space=pltpu.HBM),) * 2,
                scratch_shapes=[pltpu.SemaphoreType.DMA((2,))],
            )(filtered, margin)
        else:
            filtered, margin = pl.pallas_call(
                functools.partial(plain_kernel, doms, bands, tuple(chunks)),
                out_shape=(
                    jax.ShapeDtypeStruct((nodes, cols), BF16),
                    jax.ShapeDtypeStruct((1, cols, bands * cols), F32),
                ),
                in_specs=[pl.BlockSpec(memory_space=pltpu.HBM)] * 5,
                out_specs=(pl.BlockSpec(memory_space=pltpu.VMEM),) * 2,
                scratch_shapes=[
                    pltpu.SMEM(cell_type.shape, jnp.int32),
                    pltpu.VMEM(cell_nodes.shape, jnp.int32),
                    pltpu.VMEM(shared_nodes.shape, jnp.int32),
                    pltpu.VMEM(vectors.shape, BF16),
                    pltpu.VMEM(cell_ham.shape, BF16),
                    pltpu.VMEM((cell_nodes.shape[0], slots, slots), BF16),
                    pltpu.VMEM((2, rim, cols), BF16),
                    pltpu.VMEM((2, rim, cols), BF16),
                    pltpu.VMEM((2, 2, rim, cols), BF16),
                    pltpu.VMEM((2, 2, rim, cols), BF16),
                    pltpu.VMEM((2, rim, cols), BF16),
                    pltpu.VMEM((2, rim, cols), BF16),
                    pltpu.VMEM((max(bands - 1, 1), nodes, cols), BF16),
                ]
                + [pltpu.SemaphoreType.DMA((5,))]
                + [pltpu.SemaphoreType.DMA((len(chunks), 2))] * 6
                + [pltpu.SemaphoreType.DMA((len(chunks), bands))] * 2,
                compiler_params=pltpu.CompilerParams(
                    collective_id=0, has_side_effects=True, vmem_limit_bytes=48 << 20
                ),
            )(*operands)
            margin = inverse_count * lax.psum_scatter(
                margin, "dom", scatter_dimension=1, tiled=True
            )
        return filtered, margin

    in_specs = (P("dom", "band"), P(), P("dom"), P("dom", None), P("dom", None))
    out_specs = (P("dom", "band"), P("band", "dom", None))
    return jax.shard_map(
        on_device, mesh=mesh, in_specs=in_specs, out_specs=out_specs, check_vma=False
    )
```

```python
import functools

import jax
import jax.numpy as jnp
from jax import lax
from jax.experimental import pallas as pl
from jax.experimental.pallas import tpu as pltpu
from jax.sharding import PartitionSpec as P

SHIFT = 0.5
INV_HALF = 0.5
GROUP = 4
WIDTHS = (128, 128, 128)
PIECES = ((0, 0, 256, 0), (0, 256, 384, 1), (1, 0, 256, 0), (1, 256, 384, 1))
ORDER = (0, 2, 1, 3)
MESH = pl.DeviceIdType.MESH
F32 = jnp.float32
BF16 = jnp.bfloat16


def dot(a, b):
    return jnp.dot(a, b, preferred_element_type=F32)


def dot_tn(a, b):
    return lax.dot_general(a, b, (((0,), (0,)), ((), ())), preferred_element_type=F32)


def dot_nt(a, b):
    return lax.dot_general(a, b, (((1,), (1,)), ((), ())), preferred_element_type=F32)


def one_hot(rows, index_row):
    spots = lax.broadcasted_iota(jnp.int32, (rows, index_row.shape[1]), 0)
    return jnp.where(spots == index_row, 1.0, 0.0).astype(BF16)


def kernel(
    doms, bands, chunks, inverse_count,
    type_hbm, nodes_hbm, shared_hbm, v_hbm, ham_hbm,
    filt_ref, margin_ref,
    type_ref, nodes_ref, shared_ref, v_ref, ham, hp,
    perm, v_own, base, first_ref, filt, product_ref,
    send1, ghost, send2, recv2, send3, recv3, everyone,
    in_sem, s1, r1, s2, r2, s3, r3, s4, r4, known,
    *held_refs,
):
    dom = lax.axis_index("dom")
    band = lax.axis_index("band")
    nodes, cols = v_ref.shape
    cells = nodes_ref.shape[0]
    rim = shared_ref.shape[1] // 2
    edge = 2 * rim
    slots = nodes + edge
    present = (dom > 0, dom < doms - 1)
    beside = (jnp.maximum(dom - 1, 0), jnp.minimum(dom + 1, doms - 1))

    load_shared, load_v, load_nodes, load_type, load_ham = [
        pltpu.make_async_copy(source, target, in_sem.at[number])
        for number, (source, target) in enumerate(
            (
                (shared_hbm, shared_ref),
                (v_hbm, v_ref),
                (nodes_hbm, nodes_ref),
                (type_hbm, type_ref),
                (ham_hbm, ham),
            )
        )
    ]

    for load in (load_shared, load_v, load_nodes, load_type, load_ham):
        load.start()
    barrier = pltpu.get_barrier_semaphore()

    def greet(other_dom, other_band):
        pl.semaphore_signal(
            barrier, inc=1,
            device_id={"dom": other_dom, "band": other_band},
            device_id_type=MESH,
        )

    for side in (0, 1):
        @pl.when(present[side])
        def _():
            greet(beside[side], band)
    for step in range(1, bands):
        greet(dom, lax.rem(band + step, bands))

    for side in (0, 1):
        @pl.when(jnp.logical_not(present[side]))
        def _():
            ghost[side] = jnp.zeros((rim, cols), BF16)
            recv2[side] = jnp.zeros((2, rim, cols), BF16)
            recv3[side] = jnp.zeros((rim, cols), BF16)

    far = lax.rem(dom, 2)
    in_order = ((far, dom + 2 * far - 1), (1 - far, dom + 1 - 2 * far))

    def swap(source, target, sent, got, chunk, side, other, arriving):
        low, high = chunks[chunk]
        landing = side if arriving else 1 - side
        return pltpu.make_async_remote_copy(
            src_ref=source.at[side, ..., low:high],
            dst_ref=target.at[landing, ..., low:high],
            send_sem=sent.at[chunk, side],
            recv_sem=got.at[chunk, landing],
            device_id={"dom": other, "band": band},
            device_id_type=MESH,
        )

    def swap_start(*args):
        for side, other in in_order:
            @pl.when(jnp.logical_and(other >= 0, other < doms))
            def _():
                swap(*args, side, other, False).start()

    def swap_wait(*args):
        for side in (0, 1):
            @pl.when(present[side])
            def _():
                swap(*args, side, beside[side], True).wait()

    load_shared.wait()
    load_v.wait()
    pick = one_hot(nodes, shared_ref[...])
    send1[...] = dot_tn(pick, v_ref[...]).astype(BF16).reshape(2, rim, cols)

    pl.semaphore_wait(
        barrier,
        bands - 1 + jnp.where(present[0], 1, 0) + jnp.where(present[1], 1, 0),
    )
    numbers = range(len(chunks))
    for chunk in numbers:
        swap_start(send1, ghost, s1, r1, chunk)

    free = 1.0 - jnp.sum(pick.astype(F32), axis=1, keepdims=True)
    below = lax.broadcasted_iota(jnp.int32, (nodes, nodes), 0) > lax.broadcasted_iota(
        jnp.int32, (nodes, nodes), 1
    )
    rank = dot(
        jnp.where(below, 1.0, 0.0).astype(BF16),
        jnp.broadcast_to(free, (nodes, 128)).astype(BF16),
    )[:, :1]
    spots = lax.broadcasted_iota(jnp.int32, (nodes, nodes - edge), 1).astype(F32)
    rest = jnp.where(jnp.logical_and(spots == rank, free > 0.5), 1.0, 0.0).astype(BF16)
    perm[:, :edge] = pick
    perm[:, edge:] = rest
    count = lax.broadcasted_iota(jnp.int32, (nodes, 128), 0)
    digits = jnp.where(
        lax.broadcasted_iota(jnp.int32, (nodes, 128), 1) == 0, count // 32, count % 32
    )
    digits = dot_tn(perm[...], digits.astype(BF16))
    name = (32.0 * digits[:, :1] + digits[:, 1:2]).astype(jnp.int32)
    v_own[:edge] = send1[...].reshape(edge, cols)
    v_own[edge:] = dot_tn(rest, v_ref[...]).astype(BF16)

    load_nodes.wait()
    load_type.wait()
    load_ham.wait()
    spreads = []
    for cell in range(cells):
        slot = nodes_ref[cell : cell + 1, :]
        slot = jnp.where(slot < rim, slot + nodes, jnp.where(slot < nodes + rim, slot - rim, slot))
        outside = lax.broadcasted_iota(jnp.int32, (edge, slot.shape[1]), 0) + nodes
        spreads.append([
            jnp.where(rows == slot, 1.0, 0.0).astype(BF16)
            for rows in (name[:edge], name[edge:], outside)
        ])

    def assemble(rows, part):
        for cell in range(cells):
            wanted = dot(spreads[cell][part], ham[type_ref[cell]]).astype(BF16)
            hp[cell, rows[0] : rows[1]] = dot_nt(
                wanted, jnp.concatenate(spreads[cell], axis=0)
            ).astype(BF16)

    def apply(rows, columns, field):
        total = dot(hp[0, rows[0] : rows[1], columns[0] : columns[1]], field)
        for cell in range(1, cells):
            total += dot(hp[cell, rows[0] : rows[1], columns[0] : columns[1]], field)
        return total

    on_edge, inner, owned, outer = (0, edge), (edge, nodes), (0, nodes), (nodes, slots)
    assemble(outer, 2)
    base[nodes:] = apply(outer, owned, v_own[...])
    assemble(on_edge, 0)
    base[:edge] = apply(on_edge, owned, v_own[...])

    held = []
    for chunk, (low, high) in enumerate(chunks):
        wide = high - low
        swap_wait(send1, ghost, s1, r1, chunk)
        rims = ghost[:, :, low:high].reshape(edge, wide)
        y_rim = base[nodes:, low:high] + apply(outer, outer, rims)
        send2[:, 0, :, low:high] = y_rim.astype(BF16).reshape(2, rim, wide)
        y_edge = base[:edge, low:high] + apply(on_edge, outer, rims)
        send2[:, 1, :, low:high] = y_edge.astype(BF16).reshape(2, rim, wide)
        swap_start(send2, recv2, s2, r2, chunk)
        held.append((y_edge, y_rim))
    assemble(inner, 1)
    y_inner = apply(inner, owned, v_own[...]) + apply(inner, outer, ghost[...].reshape(edge, cols))
    first_ref[edge:] = ((y_inner - SHIFT * v_own[edge:].astype(F32)) * INV_HALF).astype(BF16)
    base[...] = apply((0, slots), inner, first_ref[edge:, :])

    def finish(second, first, v):
        return (2.0 * (second - SHIFT * first.astype(F32)) * INV_HALF - v.astype(F32)).astype(BF16)

    again = []
    for chunk, (low, high) in enumerate(chunks):
        wide = high - low
        y_edge, y_rim = held[chunk]
        v32 = v_own[:edge, low:high].astype(F32)
        rims = ghost[:, :, low:high].reshape(edge, wide).astype(F32)
        swap_wait(send2, recv2, s2, r2, chunk)
        y_edge = y_edge + recv2[:, 0, :, low:high].reshape(edge, wide).astype(F32)
        y_rim = y_rim + recv2[:, 1, :, low:high].reshape(edge, wide).astype(F32)
        first = ((y_edge - SHIFT * v32) * INV_HALF).astype(BF16)
        first_rim = ((y_rim - SHIFT * rims) * INV_HALF).reshape(2, rim, wide)
        first_rim = jnp.concatenate(
            [jnp.where(present[side], first_rim[side], 0.0) for side in (0, 1)], axis=0
        ).astype(BF16)
        out_rim = base[nodes:, low:high] + apply(outer, on_edge, first) + apply(outer, outer, first_rim)
        send3[:, :, low:high] = out_rim.astype(BF16).reshape(2, rim, wide)
        swap_start(send3, recv3, s3, r3, chunk)
        out = base[:nodes, low:high] + apply(owned, on_edge, first) + apply(owned, outer, first_rim)
        filt[edge:, low:high] = finish(
            out[edge:], first_ref[edge:, low:high], v_own[edge:, low:high]
        )
        again.append((out[:edge], first))

    inside, stack = lax.rem(dom, GROUP), dom // GROUP
    linked = (stack > 0, stack < doms // GROUP - 1)

    def announce(turn):
        if turn:
            hear(turn - 1)
        for side in (0, 1):
            @pl.when(linked[side])
            def _():
                pl.semaphore_signal(
                    known.at[turn, 1 - side], inc=1,
                    device_id={"dom": dom + (GROUP if side else -GROUP), "band": band},
                    device_id_type=MESH,
                )

    def hear(turn):
        for side in (0, 1):
            @pl.when(linked[side])
            def _():
                pl.semaphore_wait(known.at[turn, side], 1)

    def share(part):
        rows, (low, high) = ((edge, nodes), (0, cols)) if part == 0 else ((0, edge), chunks[part - 1])
        return pltpu.make_async_remote_copy(
            src_ref=filt.at[rows[0] : rows[1], low:high],
            dst_ref=everyone.at[rows[0] : rows[1], low:high],
            send_sem=s4.at[part],
            recv_sem=r4.at[part],
            device_id={"dom": dom, "band": 1 - band},
            device_id_type=MESH,
        )

    share(0).start()
    product_ref[0] = dot_tn(filt[edge:], filt[edge:])
    share(0).wait_recv()
    product_ref[1] = dot_tn(filt[edge:], everyone[edge:])
    for chunk, (low, high) in enumerate(chunks):
        wide = high - low
        second, first = again[chunk]
        swap_wait(send3, recv3, s3, r3, chunk)
        if chunk < 2:
            announce(chunk)
        second = second + recv3[:, :, low:high].reshape(edge, wide).astype(F32)
        filt[:edge, low:high] = finish(second, first, v_own[:edge, low:high])
        share(chunk + 1).start()

    def place(step, low, high):
        start = lax.rem(band + step, bands) * cols + low
        return pl.ds(pl.multiple_of(start, 128), high - low)

    def others(step):
        if step == 0:
            return filt[:edge]
        for chunk in numbers:
            share(chunk + 1).wait_recv()
        return everyone[:edge]

    rows = cols // doms
    where = (inside, stack)

    def device(axis, index):
        return stack * GROUP + index if axis == 0 else index * GROUP + inside

    def pass_on(axis, source, target, sent, got, away, arriving=False):
        other = lax.rem(where[axis] + away, GROUP)
        landing = away - 1 if arriving else GROUP - 1 - away
        return pltpu.make_async_remote_copy(
            src_ref=source.at[other],
            dst_ref=target.at[landing],
            send_sem=sent.at[away - 1],
            recv_sem=got.at[landing],
            device_id={"dom": device(axis, other), "band": band},
            device_id_type=MESH,
        )

    def leave(axis, *args):
        mine = where[axis]
        if axis == 0:
            targets = [
                mine + (1 - 2 * lax.rem(mine, 2)) * x + (2 - 4 * (mine // 2)) * y
                for x, y in ((1, 1), (1, 0), (0, 1))
            ]
        else:
            upper = mine // 2
            targets = [3 - 3 * upper, 2 - upper, mine + 1 - 2 * lax.rem(mine, 2)]
        for target in targets:
            pass_on(axis, *args, lax.rem(target - mine + GROUP, GROUP)).start()

    def own_rows(step, low, high, axis):
        if axis:
            start = pl.multiple_of(stack * (GROUP * rows), 8)
            return product_ref[step, pl.ds(start, GROUP * rows), low:high]
        starts = [pl.multiple_of((layer * GROUP + inside) * rows, 8) for layer in range(GROUP)]
        return jnp.concatenate(
            [product_ref[step, pl.ds(start, rows), low:high] for start in starts], axis=0
        )

    away_range = range(1, GROUP)
    works = [held_refs[number : number + 9] for number in range(0, len(held_refs), 9)]
    hear(1)
    for step in range(bands):
        product = product_ref[step] + dot_tn(filt[:edge], others(step))
        product_ref[step] = product
        for (its_step, low, high, axis), work in zip(PIECES, works):
            if its_step != step:
                continue
            part, arrived, s5, r5 = work[:4]
            for member in range(GROUP):
                if axis == 0:
                    block = jnp.concatenate(
                        [
                            product[(layer * GROUP + member) * rows : (layer * GROUP + member + 1) * rows, low:high]
                            for layer in range(GROUP)
                        ],
                        axis=0,
                    )
                else:
                    block = product[member * GROUP * rows : (member + 1) * GROUP * rows, low:high]
                part[member] = block.astype(BF16)
            leave(axis, part, arrived, s5, r5)
    filt_ref[...] = dot(perm[...], filt[...]).astype(BF16)
    for number in ORDER:
        step, low, high, axis = PIECES[number]
        part, arrived, s5, r5, part2, own_part2, arrived2, s6, r6 = works[number]
        total = own_rows(step, low, high, axis)
        for away in away_range:
            pass_on(axis, part, arrived, s5, r5, away, True).wait_recv()
            total += arrived[away - 1].astype(F32)
        for layer in range(GROUP):
            block = total[layer * rows : (layer + 1) * rows]
            own_part2[layer] = block
            part2[layer] = block.astype(BF16)
        leave(1 - axis, part2, arrived2, s6, r6)
    for number in ORDER:
        step, low, high, axis = PIECES[number]
        part, arrived, s5, r5, part2, own_part2, arrived2, s6, r6 = works[number]
        total = own_part2[where[1 - axis]]
        for away in away_range:
            pass_on(1 - axis, part2, arrived2, s6, r6, away, True).wait_recv()
            total += arrived2[away - 1].astype(F32)
        margin_ref[0, :, place(step, low, high)] = total * inverse_count
    for number, (step, low, high, axis) in enumerate(PIECES):
        part, arrived, s5, r5, part2, own_part2, arrived2, s6, r6 = works[number]
        for away in away_range:
            pass_on(axis, part, arrived, s5, r5, away).wait_send()
            pass_on(1 - axis, part2, arrived2, s6, r6, away).wait_send()
    for part in range(len(chunks) + 1):
        share(part).wait_send()


def plain_kernel(
    doms, bands, chunks,
    type_hbm, nodes_hbm, shared_hbm, v_hbm, ham_hbm,
    filt_ref, margin_ref,
    type_ref, nodes_ref, shared_ref, v_ref, ham, hp,
    send1, ghost, send2, recv2, send3, recv3, everyone,
    in_sem, s1, r1, s2, r2, s3, r3, s4, r4,
):
    dom = lax.axis_index("dom")
    band = lax.axis_index("band")
    nodes, cols = v_ref.shape
    cells = nodes_ref.shape[0]
    rim = shared_ref.shape[1] // 2
    slots = nodes + 2 * rim
    present = (dom > 0, dom < doms - 1)
    beside = (jnp.maximum(dom - 1, 0), jnp.minimum(dom + 1, doms - 1))

    load_shared, load_v, load_nodes, load_type, load_ham = [
        pltpu.make_async_copy(source, target, in_sem.at[number])
        for number, (source, target) in enumerate(
            (
                (shared_hbm, shared_ref),
                (v_hbm, v_ref),
                (nodes_hbm, nodes_ref),
                (type_hbm, type_ref),
                (ham_hbm, ham),
            )
        )
    ]

    barrier = pltpu.get_barrier_semaphore()

    def greet(other_dom, other_band):
        pl.semaphore_signal(
            barrier, inc=1,
            device_id={"dom": other_dom, "band": other_band},
            device_id_type=MESH,
        )

    for side in (0, 1):
        @pl.when(present[side])
        def _():
            greet(beside[side], band)
    for step in range(1, bands):
        greet(dom, lax.rem(band + step, bands))
    for load in (load_shared, load_v, load_nodes, load_type, load_ham):
        load.start()

    for side in (0, 1):
        @pl.when(jnp.logical_not(present[side]))
        def _():
            ghost[side] = jnp.zeros((rim, cols), BF16)
            recv2[side] = jnp.zeros((2, rim, cols), BF16)
            recv3[side] = jnp.zeros((rim, cols), BF16)

    def swap(source, target, sent, got, chunk, side, arriving):
        low, high = chunks[chunk]
        landing = side if arriving else 1 - side
        return pltpu.make_async_remote_copy(
            src_ref=source.at[side, ..., low:high],
            dst_ref=target.at[landing, ..., low:high],
            send_sem=sent.at[chunk, side],
            recv_sem=got.at[chunk, landing],
            device_id={"dom": beside[side], "band": band},
            device_id_type=MESH,
        )

    def swap_start(*args):
        for side in (0, 1):
            @pl.when(present[side])
            def _():
                swap(*args, side, False).start()

    def swap_wait(*args):
        for side in (0, 1):
            @pl.when(present[side])
            def _():
                swap(*args, side, True).wait()

    load_shared.wait()
    load_v.wait()
    pick = one_hot(nodes, shared_ref[...])
    send1[...] = dot_tn(pick, v_ref[...]).astype(BF16).reshape(2, rim, cols)

    pl.semaphore_wait(
        barrier,
        bands - 1 + jnp.where(present[0], 1, 0) + jnp.where(present[1], 1, 0),
    )
    numbers = range(len(chunks))
    for chunk in numbers:
        swap_start(send1, ghost, s1, r1, chunk)

    load_nodes.wait()
    load_type.wait()
    load_ham.wait()
    for cell in range(cells):
        slot = nodes_ref[cell : cell + 1, :]
        slot = jnp.where(slot < rim, slot + nodes, jnp.where(slot < nodes + rim, slot - rim, slot))
        spread = one_hot(slots, slot)
        spread_ham = dot(spread, ham[type_ref[cell]]).astype(BF16)
        hp[cell] = dot_nt(spread_ham, spread).astype(BF16)

    def apply(low, high, own, rims):
        total = dot(hp[0, low:high, :nodes], own) + dot(hp[0, low:high, nodes:], rims)
        for cell in range(1, cells):
            total += dot(hp[cell, low:high, :nodes], own) + dot(hp[cell, low:high, nodes:], rims)
        return total

    held = []
    for chunk, (low, high) in enumerate(chunks):
        wide = high - low
        swap_wait(send1, ghost, s1, r1, chunk)
        v = v_ref[:, low:high]
        rims = ghost[:, :, low:high].reshape(2 * rim, wide)
        y_own = apply(0, nodes, v, rims)
        send2[:, 1, :, low:high] = (
            dot_tn(pick, y_own.astype(BF16)).astype(BF16).reshape(2, rim, wide)
        )
        y_rim = apply(nodes, slots, v, rims)
        send2[:, 0, :, low:high] = y_rim.astype(BF16).reshape(2, rim, wide)
        swap_start(send2, recv2, s2, r2, chunk)
        held.append((y_own, y_rim))

    again = []
    for chunk, (low, high) in enumerate(chunks):
        wide = high - low
        y_own, y_rim = held[chunk]
        v32 = v_ref[:, low:high].astype(F32)
        rims = ghost[:, :, low:high].reshape(2 * rim, wide).astype(F32)
        swap_wait(send2, recv2, s2, r2, chunk)
        y_own = y_own + dot(pick, recv2[:, 0, :, low:high].reshape(2 * rim, wide))
        y_rim = y_rim + recv2[:, 1, :, low:high].reshape(2 * rim, wide).astype(F32)
        first = ((y_own - SHIFT * v32) * INV_HALF).astype(BF16)
        first_rim = ((y_rim - SHIFT * rims) * INV_HALF).reshape(2, rim, wide)
        first_rim = jnp.concatenate(
            [jnp.where(present[side], first_rim[side], 0.0) for side in (0, 1)], axis=0
        ).astype(BF16)
        out_rim = apply(nodes, slots, first, first_rim)
        send3[:, :, low:high] = out_rim.astype(BF16).reshape(2, rim, wide)
        swap_start(send3, recv3, s3, r3, chunk)
        again.append((apply(0, nodes, first, first_rim), first))

    def share(chunk, step, arriving=False):
        low, high = chunks[chunk]
        landing = step - 1 if arriving else bands - 1 - step
        return pltpu.make_async_remote_copy(
            src_ref=filt_ref.at[:, low:high],
            dst_ref=everyone.at[landing, :, low:high],
            send_sem=s4.at[chunk, step],
            recv_sem=r4.at[chunk, landing],
            device_id={"dom": dom, "band": lax.rem(band + step, bands)},
            device_id_type=MESH,
        )

    for chunk, (low, high) in enumerate(chunks):
        wide = high - low
        second, first = again[chunk]
        v32 = v_ref[:, low:high].astype(F32)
        swap_wait(send3, recv3, s3, r3, chunk)
        second = second + dot(pick, recv3[:, :, low:high].reshape(2 * rim, wide))
        filt_ref[:, low:high] = (
            2.0 * (second - SHIFT * first.astype(F32)) * INV_HALF - v32
        ).astype(BF16)
        for step in range(1, bands):
            share(chunk, step).start()

    def place(step):
        return pl.ds(pl.multiple_of(lax.rem(band + step, bands) * cols, 128), cols)

    for step in range(bands):
        if step == 0:
            other = filt_ref[...]
        else:
            for chunk in numbers:
                share(chunk, step, True).wait_recv()
            other = everyone[step - 1]
        product = dot_tn(filt_ref[...], other)
        margin_ref[0, :, place(step)] = product
    for chunk in numbers:
        for step in range(1, bands):
            share(chunk, step).wait_send()


def put_out(filt_ref, margin_ref, filt_hbm, margin_hbm, sem):
    copies = [
        pltpu.make_async_copy(source, target, sem.at[number])
        for number, (source, target) in enumerate(
            ((filt_ref, filt_hbm), (margin_ref, margin_hbm))
        )
    ]
    for copy in copies:
        copy.start()
    for copy in copies:
        copy.wait()


def solution(mesh):
    doms, bands = mesh.shape["dom"], mesh.shape["band"]

    def on_device(vectors, cell_ham, cell_type, cell_nodes, shared_nodes):
        nodes, cols = vectors.shape
        rim = shared_nodes.shape[1] // 2
        slots = nodes + 2 * rim
        rows = cols // doms
        scatter_here = cols % doms == 0 and rows % 8 == 0 and doms == GROUP * GROUP and bands == 2
        inverse_count = 1.0 / (nodes * doms)
        chunks = []
        for width in WIDTHS + (cols,):
            low = chunks[-1][1] if chunks else 0
            if low < cols:
                chunks.append((low, min(low + width, cols)))
        kept = []
        if scatter_here:
            for _, low, high, _ in PIECES:
                wide = high - low
                kept += [
                    pltpu.VMEM((GROUP, GROUP * rows, wide), BF16),
                    pltpu.VMEM((GROUP - 1, GROUP * rows, wide), BF16),
                ]
                kept += [pltpu.SemaphoreType.DMA((GROUP - 1,))] * 2
                kept += [
                    pltpu.VMEM((GROUP, rows, wide), BF16),
                    pltpu.VMEM((GROUP, rows, wide), F32),
                    pltpu.VMEM((GROUP - 1, rows, wide), BF16),
                ]
                kept += [pltpu.SemaphoreType.DMA((GROUP - 1,))] * 2
        operands = [
            pltpu.with_memory_space_constraint(operand, pltpu.HBM)
            for operand in (cell_type, cell_nodes, shared_nodes, vectors, cell_ham)
        ]
        if scatter_here:
            filtered, margin = pl.pallas_call(
                functools.partial(kernel, doms, bands, tuple(chunks), inverse_count),
                out_shape=(
                    jax.ShapeDtypeStruct((nodes, cols), BF16),
                    jax.ShapeDtypeStruct((1, rows, bands * cols), F32),
                ),
                in_specs=[pl.BlockSpec(memory_space=pltpu.HBM)] * 5,
                out_specs=(pl.BlockSpec(memory_space=pltpu.VMEM),) * 2,
                scratch_shapes=[
                    pltpu.SMEM(cell_type.shape, jnp.int32),
                    pltpu.VMEM(cell_nodes.shape, jnp.int32),
                    pltpu.VMEM(shared_nodes.shape, jnp.int32),
                    pltpu.VMEM(vectors.shape, BF16),
                    pltpu.VMEM(cell_ham.shape, BF16),
                    pltpu.VMEM((cell_nodes.shape[0], slots, slots), BF16),
                    pltpu.VMEM((nodes, nodes), BF16),
                    pltpu.VMEM((nodes, cols), BF16),
                    pltpu.VMEM((slots, cols), F32),
                    pltpu.VMEM((nodes, cols), BF16),
                    pltpu.VMEM((nodes, cols), BF16),
                    pltpu.VMEM((bands, cols, cols), F32),
                    pltpu.VMEM((2, rim, cols), BF16),
                    pltpu.VMEM((2, rim, cols), BF16),
                    pltpu.VMEM((2, 2, rim, cols), BF16),
                    pltpu.VMEM((2, 2, rim, cols), BF16),
                    pltpu.VMEM((2, rim, cols), BF16),
                    pltpu.VMEM((2, rim, cols), BF16),
                    pltpu.VMEM((nodes, cols), BF16),
                ]
                + [pltpu.SemaphoreType.DMA((5,))]
                + [pltpu.SemaphoreType.DMA((len(chunks), 2))] * 6
                + [pltpu.SemaphoreType.DMA((len(chunks) + 1,))] * 2
                + [pltpu.SemaphoreType.REGULAR((2, 2))]
                + kept,
                compiler_params=pltpu.CompilerParams(
                    collective_id=0, has_side_effects=True, vmem_limit_bytes=48 << 20
                ),
            )(*operands)
            filtered, margin = [
                pltpu.with_memory_space_constraint(result, pltpu.VMEM)
                for result in (filtered, margin)
            ]
            filtered, margin = pl.pallas_call(
                put_out,
                out_shape=(
                    jax.ShapeDtypeStruct(filtered.shape, BF16),
                    jax.ShapeDtypeStruct(margin.shape, F32),
                ),
                in_specs=[pl.BlockSpec(memory_space=pltpu.VMEM)] * 2,
                out_specs=(pl.BlockSpec(memory_space=pltpu.HBM),) * 2,
                scratch_shapes=[pltpu.SemaphoreType.DMA((2,))],
            )(filtered, margin)
        else:
            filtered, margin = pl.pallas_call(
                functools.partial(plain_kernel, doms, bands, tuple(chunks)),
                out_shape=(
                    jax.ShapeDtypeStruct((nodes, cols), BF16),
                    jax.ShapeDtypeStruct((1, cols, bands * cols), F32),
                ),
                in_specs=[pl.BlockSpec(memory_space=pltpu.HBM)] * 5,
                out_specs=(pl.BlockSpec(memory_space=pltpu.VMEM),) * 2,
                scratch_shapes=[
                    pltpu.SMEM(cell_type.shape, jnp.int32),
                    pltpu.VMEM(cell_nodes.shape, jnp.int32),
                    pltpu.VMEM(shared_nodes.shape, jnp.int32),
                    pltpu.VMEM(vectors.shape, BF16),
                    pltpu.VMEM(cell_ham.shape, BF16),
                    pltpu.VMEM((cell_nodes.shape[0], slots, slots), BF16),
                    pltpu.VMEM((2, rim, cols), BF16),
                    pltpu.VMEM((2, rim, cols), BF16),
                    pltpu.VMEM((2, 2, rim, cols), BF16),
                    pltpu.VMEM((2, 2, rim, cols), BF16),
                    pltpu.VMEM((2, rim, cols), BF16),
                    pltpu.VMEM((2, rim, cols), BF16),
                    pltpu.VMEM((max(bands - 1, 1), nodes, cols), BF16),
                ]
                + [pltpu.SemaphoreType.DMA((5,))]
                + [pltpu.SemaphoreType.DMA((len(chunks), 2))] * 6
                + [pltpu.SemaphoreType.DMA((len(chunks), bands))] * 2,
                compiler_params=pltpu.CompilerParams(
                    collective_id=0, has_side_effects=True, vmem_limit_bytes=48 << 20
                ),
            )(*operands)
            margin = inverse_count * lax.psum_scatter(
                margin, "dom", scatter_dimension=1, tiled=True
            )
        return filtered, margin

    in_specs = (P("dom", "band"), P(), P("dom"), P("dom", None), P("dom", None))
    out_specs = (P("dom", "band"), P("band", "dom", None))
    return jax.shard_map(
        on_device, mesh=mesh, in_specs=in_specs, out_specs=out_specs, check_vma=False
    )
```

```python
import functools

import jax
import jax.numpy as jnp
from jax import lax
from jax.experimental import pallas as pl
from jax.experimental.pallas import tpu as pltpu
from jax.sharding import PartitionSpec as P

SHIFT = 0.5
INV_HALF = 0.5
GROUP = 4
WIDTHS = (128, 128, 128)
PIECES = ((0, 0, 256, 0), (0, 256, 384, 1), (1, 0, 256, 0), (1, 256, 384, 1))
ORDER = (0, 2, 1, 3)
MESH = pl.DeviceIdType.MESH
F32 = jnp.float32
BF16 = jnp.bfloat16


def dot(a, b):
    return jnp.dot(a, b, preferred_element_type=F32)


def dot_tn(a, b):
    return lax.dot_general(a, b, (((0,), (0,)), ((), ())), preferred_element_type=F32)


def dot_nt(a, b):
    return lax.dot_general(a, b, (((1,), (1,)), ((), ())), preferred_element_type=F32)


def one_hot(rows, index_row):
    spots = lax.broadcasted_iota(jnp.int32, (rows, index_row.shape[1]), 0)
    return jnp.where(spots == index_row, 1.0, 0.0).astype(BF16)


def kernel(
    doms, bands, chunks, inverse_count,
    type_hbm, nodes_hbm, shared_hbm, v_hbm, ham_hbm,
    filt_ref, margin_ref,
    type_ref, nodes_ref, shared_ref, v_ref, ham, hp,
    perm, v_own, base, first_ref, filt, product_ref,
    send1, ghost, send2, recv2, send3, recv3, everyone,
    in_sem, s1, r1, s2, r2, s3, r3, s4, r4, known,
    *held_refs,
):
    dom = lax.axis_index("dom")
    band = lax.axis_index("band")
    nodes, cols = v_ref.shape
    cells = nodes_ref.shape[0]
    rim = shared_ref.shape[1] // 2
    edge = 2 * rim
    slots = nodes + edge
    present = (dom > 0, dom < doms - 1)
    beside = (jnp.maximum(dom - 1, 0), jnp.minimum(dom + 1, doms - 1))

    load_shared, load_v, load_nodes, load_type, load_ham = [
        pltpu.make_async_copy(source, target, in_sem.at[number])
        for number, (source, target) in enumerate(
            (
                (shared_hbm, shared_ref),
                (v_hbm, v_ref),
                (nodes_hbm, nodes_ref),
                (type_hbm, type_ref),
                (ham_hbm, ham),
            )
        )
    ]

    for load in (load_shared, load_v, load_nodes, load_type, load_ham):
        load.start()
    barrier = pltpu.get_barrier_semaphore()

    def greet(other_dom, other_band):
        pl.semaphore_signal(
            barrier, inc=1,
            device_id={"dom": other_dom, "band": other_band},
            device_id_type=MESH,
        )

    for side in (0, 1):
        @pl.when(present[side])
        def _():
            greet(beside[side], band)
    for step in range(1, bands):
        greet(dom, lax.rem(band + step, bands))

    for side in (0, 1):
        @pl.when(jnp.logical_not(present[side]))
        def _():
            ghost[side] = jnp.zeros((rim, cols), BF16)
            recv2[side] = jnp.zeros((2, rim, cols), BF16)
            recv3[side] = jnp.zeros((rim, cols), BF16)

    far = lax.rem(dom, 2)
    in_order = ((far, dom + 2 * far - 1), (1 - far, dom + 1 - 2 * far))

    def swap(source, target, sent, got, chunk, side, other, arriving):
        low, high = chunks[chunk]
        landing = side if arriving else 1 - side
        return pltpu.make_async_remote_copy(
            src_ref=source.at[side, ..., low:high],
            dst_ref=target.at[landing, ..., low:high],
            send_sem=sent.at[chunk, side],
            recv_sem=got.at[chunk, landing],
            device_id={"dom": other, "band": band},
            device_id_type=MESH,
        )

    def swap_start(*args):
        for side, other in in_order:
            @pl.when(jnp.logical_and(other >= 0, other < doms))
            def _():
                swap(*args, side, other, False).start()

    def swap_wait(*args):
        for side in (0, 1):
            @pl.when(present[side])
            def _():
                swap(*args, side, beside[side], True).wait()

    load_shared.wait()
    load_v.wait()
    pick = one_hot(nodes, shared_ref[...])
    send1[...] = dot_tn(pick, v_ref[...]).astype(BF16).reshape(2, rim, cols)

    pl.semaphore_wait(
        barrier,
        bands - 1 + jnp.where(present[0], 1, 0) + jnp.where(present[1], 1, 0),
    )
    numbers = range(len(chunks))
    for chunk in numbers:
        swap_start(send1, ghost, s1, r1, chunk)

    free = 1.0 - jnp.sum(pick.astype(F32), axis=1, keepdims=True)
    below = lax.broadcasted_iota(jnp.int32, (nodes, nodes), 0) > lax.broadcasted_iota(
        jnp.int32, (nodes, nodes), 1
    )
    rank = dot(
        jnp.where(below, 1.0, 0.0).astype(BF16),
        jnp.broadcast_to(free, (nodes, 128)).astype(BF16),
    )[:, :1]
    spots = lax.broadcasted_iota(jnp.int32, (nodes, nodes - edge), 1).astype(F32)
    rest = jnp.where(jnp.logical_and(spots == rank, free > 0.5), 1.0, 0.0).astype(BF16)
    perm[:, :edge] = pick
    perm[:, edge:] = rest
    count = lax.broadcasted_iota(jnp.int32, (nodes, 128), 0)
    digits = jnp.where(
        lax.broadcasted_iota(jnp.int32, (nodes, 128), 1) == 0, count // 32, count % 32
    )
    digits = dot_tn(perm[...], digits.astype(BF16))
    name = (32.0 * digits[:, :1] + digits[:, 1:2]).astype(jnp.int32)
    v_own[:edge] = send1[...].reshape(edge, cols)
    v_own[edge:] = dot_tn(rest, v_ref[...]).astype(BF16)

    load_nodes.wait()
    load_type.wait()
    load_ham.wait()
    spreads = []
    for cell in range(cells):
        slot = nodes_ref[cell : cell + 1, :]
        slot = jnp.where(slot < rim, slot + nodes, jnp.where(slot < nodes + rim, slot - rim, slot))
        outside = lax.broadcasted_iota(jnp.int32, (edge, slot.shape[1]), 0) + nodes
        spreads.append([
            jnp.where(rows == slot, 1.0, 0.0).astype(BF16)
            for rows in (name[:edge], name[edge:], outside)
        ])

    def assemble(rows, part):
        for cell in range(cells):
            wanted = dot(spreads[cell][part], ham[type_ref[cell]]).astype(BF16)
            hp[cell, rows[0] : rows[1]] = dot_nt(
                wanted, jnp.concatenate(spreads[cell], axis=0)
            ).astype(BF16)

    def apply(rows, columns, field):
        total = dot(hp[0, rows[0] : rows[1], columns[0] : columns[1]], field)
        for cell in range(1, cells):
            total += dot(hp[cell, rows[0] : rows[1], columns[0] : columns[1]], field)
        return total

    on_edge, inner, owned, outer = (0, edge), (edge, nodes), (0, nodes), (nodes, slots)
    assemble(outer, 2)
    base[nodes:] = apply(outer, owned, v_own[...])
    assemble(on_edge, 0)
    base[:edge] = apply(on_edge, owned, v_own[...])

    held = []
    for chunk, (low, high) in enumerate(chunks):
        wide = high - low
        swap_wait(send1, ghost, s1, r1, chunk)
        rims = ghost[:, :, low:high].reshape(edge, wide)
        y_rim = base[nodes:, low:high] + apply(outer, outer, rims)
        send2[:, 0, :, low:high] = y_rim.astype(BF16).reshape(2, rim, wide)
        y_edge = base[:edge, low:high] + apply(on_edge, outer, rims)
        send2[:, 1, :, low:high] = y_edge.astype(BF16).reshape(2, rim, wide)
        swap_start(send2, recv2, s2, r2, chunk)
        held.append((y_edge, y_rim))
    assemble(inner, 1)
    y_inner = apply(inner, owned, v_own[...]) + apply(inner, outer, ghost[...].reshape(edge, cols))
    first_ref[edge:] = ((y_inner - SHIFT * v_own[edge:].astype(F32)) * INV_HALF).astype(BF16)
    base[...] = apply((0, slots), inner, first_ref[edge:, :])

    def finish(second, first, v):
        return (2.0 * (second - SHIFT * first.astype(F32)) * INV_HALF - v.astype(F32)).astype(BF16)

    again = []
    for chunk, (low, high) in enumerate(chunks):
        wide = high - low
        y_edge, y_rim = held[chunk]
        v32 = v_own[:edge, low:high].astype(F32)
        rims = ghost[:, :, low:high].reshape(edge, wide).astype(F32)
        swap_wait(send2, recv2, s2, r2, chunk)
        y_edge = y_edge + recv2[:, 0, :, low:high].reshape(edge, wide).astype(F32)
        y_rim = y_rim + recv2[:, 1, :, low:high].reshape(edge, wide).astype(F32)
        first = ((y_edge - SHIFT * v32) * INV_HALF).astype(BF16)
        first_rim = ((y_rim - SHIFT * rims) * INV_HALF).reshape(2, rim, wide)
        first_rim = jnp.concatenate(
            [jnp.where(present[side], first_rim[side], 0.0) for side in (0, 1)], axis=0
        ).astype(BF16)
        out_rim = base[nodes:, low:high] + apply(outer, on_edge, first) + apply(outer, outer, first_rim)
        send3[:, :, low:high] = out_rim.astype(BF16).reshape(2, rim, wide)
        swap_start(send3, recv3, s3, r3, chunk)
        out = base[:nodes, low:high] + apply(owned, on_edge, first) + apply(owned, outer, first_rim)
        filt[edge:, low:high] = finish(
            out[edge:], first_ref[edge:, low:high], v_own[edge:, low:high]
        )
        again.append((out[:edge], first))

    inside, stack = lax.rem(dom, GROUP), dom // GROUP
    linked = (stack > 0, stack < doms // GROUP - 1)

    def announce(turn):
        if turn:
            hear(turn - 1)
        for side in (0, 1):
            @pl.when(linked[side])
            def _():
                pl.semaphore_signal(
                    known.at[turn, 1 - side], inc=1,
                    device_id={"dom": dom + (GROUP if side else -GROUP), "band": band},
                    device_id_type=MESH,
                )

    def hear(turn):
        for side in (0, 1):
            @pl.when(linked[side])
            def _():
                pl.semaphore_wait(known.at[turn, side], 1)

    def share(part):
        rows, (low, high) = ((edge, nodes), (0, cols)) if part == 0 else ((0, edge), chunks[part - 1])
        return pltpu.make_async_remote_copy(
            src_ref=filt.at[rows[0] : rows[1], low:high],
            dst_ref=everyone.at[rows[0] : rows[1], low:high],
            send_sem=s4.at[part],
            recv_sem=r4.at[part],
            device_id={"dom": dom, "band": 1 - band},
            device_id_type=MESH,
        )

    share(0).start()
    product_ref[0] = dot_tn(filt[edge:], filt[edge:])
    share(0).wait_recv()
    product_ref[1] = dot_tn(filt[edge:], everyone[edge:])
    def place(step, low, high):
        start = lax.rem(band + step, bands) * cols + low
        return pl.ds(pl.multiple_of(start, 128), high - low)

    def others(step):
        if step == 0:
            return filt[:edge]
        for chunk in numbers[2:]:
            share(chunk + 1).wait_recv()
        return everyone[:edge]

    rows = cols // doms
    where = (inside, stack)

    def device(axis, index):
        return stack * GROUP + index if axis == 0 else index * GROUP + inside

    def pass_on(axis, source, target, sent, got, away, arriving=False, half=None):
        other = lax.rem(where[axis] + away, GROUP)
        landing = away - 1 if arriving else GROUP - 1 - away
        cut, shift = 2 * rows, (GROUP - 1 if half else 0)
        return pltpu.make_async_remote_copy(
            src_ref=source.at[other] if half is None else source.at[other, half * cut : (half + 1) * cut],
            dst_ref=target.at[landing] if half is None else target.at[landing, half * cut : (half + 1) * cut],
            send_sem=sent.at[away - 1 + shift],
            recv_sem=got.at[landing + shift],
            device_id={"dom": device(axis, other), "band": band},
            device_id_type=MESH,
        )

    def leave(axis, *args, half=None):
        mine = where[axis]
        if axis == 0:
            targets = [
                mine + (1 - 2 * lax.rem(mine, 2)) * x + (2 - 4 * (mine // 2)) * y
                for x, y in ((1, 1), (1, 0), (0, 1))
            ]
        else:
            upper = mine // 2
            targets = [3 - 3 * upper, 2 - upper, mine + 1 - 2 * lax.rem(mine, 2)]
        for target in targets:
            pass_on(axis, *args, lax.rem(target - mine + GROUP, GROUP), half=half).start()

    def own_rows(step, low, high, axis):
        if axis:
            start = pl.multiple_of(stack * (GROUP * rows), 8)
            return product_ref[step, pl.ds(start, GROUP * rows), low:high]
        starts = [pl.multiple_of((layer * GROUP + inside) * rows, 8) for layer in range(GROUP)]
        return jnp.concatenate(
            [product_ref[step, pl.ds(start, rows), low:high] for start in starts], axis=0
        )

    away_range = range(1, GROUP)
    works = [held_refs[number : number + 9] for number in range(0, len(held_refs), 9)]
    ready = chunks[1][1]
    ahead = GROUP * rows * 2

    def early(step):
        other = filt if step == 0 else everyone
        product = product_ref[step, :ahead, :ready] + dot_tn(filt[:edge, :ahead], other[:edge, :ready])
        for (its_step, low, high, axis), work in zip(PIECES, works):
            if its_step == step and axis == 0 and high <= ready:
                part, arrived, s5, r5 = work[:4]
                for member in range(GROUP):
                    part[member, : 2 * rows] = jnp.concatenate(
                        [
                            product[(layer * GROUP + member) * rows : (layer * GROUP + member + 1) * rows, low:high]
                            for layer in range(2)
                        ],
                        axis=0,
                    ).astype(BF16)
                leave(axis, part, arrived, s5, r5, half=0)

    for chunk, (low, high) in enumerate(chunks):
        wide = high - low
        second, first = again[chunk]
        swap_wait(send3, recv3, s3, r3, chunk)
        if chunk < 2:
            announce(chunk)
        second = second + recv3[:, :, low:high].reshape(edge, wide).astype(F32)
        filt[:edge, low:high] = finish(second, first, v_own[:edge, low:high])
        share(chunk + 1).start()
        if chunk == 1:
            early(0)
    hear(1)
    for step in range(bands):
        product = product_ref[step] + dot_tn(filt[:edge], others(step))
        product_ref[step] = product
        for (its_step, low, high, axis), work in zip(PIECES, works):
            if its_step != step:
                continue
            part, arrived, s5, r5 = work[:4]
            split = axis == 0 and high <= ready
            for member in range(GROUP):
                if axis == 0:
                    block = jnp.concatenate(
                        [
                            product[(layer * GROUP + member) * rows : (layer * GROUP + member + 1) * rows, low:high]
                            for layer in range(GROUP)
                        ],
                        axis=0,
                    )
                else:
                    block = product[member * GROUP * rows : (member + 1) * GROUP * rows, low:high]
                if split:
                    part[member, 2 * rows :] = block[2 * rows :].astype(BF16)
                else:
                    part[member] = block.astype(BF16)
            leave(axis, part, arrived, s5, r5, half=1 if split else None)
        if step == 0:
            for chunk in (0, 1):
                share(chunk + 1).wait_recv()
            early(1)
    filt_ref[...] = dot(perm[...], filt[...]).astype(BF16)
    for number in ORDER:
        step, low, high, axis = PIECES[number]
        part, arrived, s5, r5, part2, own_part2, arrived2, s6, r6 = works[number]
        total = own_rows(step, low, high, axis)
        for away in away_range:
            for half in (0, 1) if axis == 0 and high <= ready else (None,):
                pass_on(axis, part, arrived, s5, r5, away, True, half).wait_recv()
            total += arrived[away - 1].astype(F32)
        for layer in range(GROUP):
            block = total[layer * rows : (layer + 1) * rows]
            own_part2[layer] = block
            part2[layer] = block.astype(BF16)
        leave(1 - axis, part2, arrived2, s6, r6)
    for number in ORDER:
        step, low, high, axis = PIECES[number]
        part, arrived, s5, r5, part2, own_part2, arrived2, s6, r6 = works[number]
        total = own_part2[where[1 - axis]]
        for away in away_range:
            pass_on(1 - axis, part2, arrived2, s6, r6, away, True).wait_recv()
            total += arrived2[away - 1].astype(F32)
        margin_ref[0, :, place(step, low, high)] = total * inverse_count
    for number, (step, low, high, axis) in enumerate(PIECES):
        part, arrived, s5, r5, part2, own_part2, arrived2, s6, r6 = works[number]
        for away in away_range:
            for half in (0, 1) if axis == 0 and high <= ready else (None,):
                pass_on(axis, part, arrived, s5, r5, away, False, half).wait_send()
            pass_on(1 - axis, part2, arrived2, s6, r6, away).wait_send()
    for part in range(len(chunks) + 1):
        share(part).wait_send()


def plain_kernel(
    doms, bands, chunks,
    type_hbm, nodes_hbm, shared_hbm, v_hbm, ham_hbm,
    filt_ref, margin_ref,
    type_ref, nodes_ref, shared_ref, v_ref, ham, hp,
    send1, ghost, send2, recv2, send3, recv3, everyone,
    in_sem, s1, r1, s2, r2, s3, r3, s4, r4,
):
    dom = lax.axis_index("dom")
    band = lax.axis_index("band")
    nodes, cols = v_ref.shape
    cells = nodes_ref.shape[0]
    rim = shared_ref.shape[1] // 2
    slots = nodes + 2 * rim
    present = (dom > 0, dom < doms - 1)
    beside = (jnp.maximum(dom - 1, 0), jnp.minimum(dom + 1, doms - 1))

    load_shared, load_v, load_nodes, load_type, load_ham = [
        pltpu.make_async_copy(source, target, in_sem.at[number])
        for number, (source, target) in enumerate(
            (
                (shared_hbm, shared_ref),
                (v_hbm, v_ref),
                (nodes_hbm, nodes_ref),
                (type_hbm, type_ref),
                (ham_hbm, ham),
            )
        )
    ]

    barrier = pltpu.get_barrier_semaphore()

    def greet(other_dom, other_band):
        pl.semaphore_signal(
            barrier, inc=1,
            device_id={"dom": other_dom, "band": other_band},
            device_id_type=MESH,
        )

    for side in (0, 1):
        @pl.when(present[side])
        def _():
            greet(beside[side], band)
    for step in range(1, bands):
        greet(dom, lax.rem(band + step, bands))
    for load in (load_shared, load_v, load_nodes, load_type, load_ham):
        load.start()

    for side in (0, 1):
        @pl.when(jnp.logical_not(present[side]))
        def _():
            ghost[side] = jnp.zeros((rim, cols), BF16)
            recv2[side] = jnp.zeros((2, rim, cols), BF16)
            recv3[side] = jnp.zeros((rim, cols), BF16)

    def swap(source, target, sent, got, chunk, side, arriving):
        low, high = chunks[chunk]
        landing = side if arriving else 1 - side
        return pltpu.make_async_remote_copy(
            src_ref=source.at[side, ..., low:high],
            dst_ref=target.at[landing, ..., low:high],
            send_sem=sent.at[chunk, side],
            recv_sem=got.at[chunk, landing],
            device_id={"dom": beside[side], "band": band},
            device_id_type=MESH,
        )

    def swap_start(*args):
        for side in (0, 1):
            @pl.when(present[side])
            def _():
                swap(*args, side, False).start()

    def swap_wait(*args):
        for side in (0, 1):
            @pl.when(present[side])
            def _():
                swap(*args, side, True).wait()

    load_shared.wait()
    load_v.wait()
    pick = one_hot(nodes, shared_ref[...])
    send1[...] = dot_tn(pick, v_ref[...]).astype(BF16).reshape(2, rim, cols)

    pl.semaphore_wait(
        barrier,
        bands - 1 + jnp.where(present[0], 1, 0) + jnp.where(present[1], 1, 0),
    )
    numbers = range(len(chunks))
    for chunk in numbers:
        swap_start(send1, ghost, s1, r1, chunk)

    load_nodes.wait()
    load_type.wait()
    load_ham.wait()
    for cell in range(cells):
        slot = nodes_ref[cell : cell + 1, :]
        slot = jnp.where(slot < rim, slot + nodes, jnp.where(slot < nodes + rim, slot - rim, slot))
        spread = one_hot(slots, slot)
        spread_ham = dot(spread, ham[type_ref[cell]]).astype(BF16)
        hp[cell] = dot_nt(spread_ham, spread).astype(BF16)

    def apply(low, high, own, rims):
        total = dot(hp[0, low:high, :nodes], own) + dot(hp[0, low:high, nodes:], rims)
        for cell in range(1, cells):
            total += dot(hp[cell, low:high, :nodes], own) + dot(hp[cell, low:high, nodes:], rims)
        return total

    held = []
    for chunk, (low, high) in enumerate(chunks):
        wide = high - low
        swap_wait(send1, ghost, s1, r1, chunk)
        v = v_ref[:, low:high]
        rims = ghost[:, :, low:high].reshape(2 * rim, wide)
        y_own = apply(0, nodes, v, rims)
        send2[:, 1, :, low:high] = (
            dot_tn(pick, y_own.astype(BF16)).astype(BF16).reshape(2, rim, wide)
        )
        y_rim = apply(nodes, slots, v, rims)
        send2[:, 0, :, low:high] = y_rim.astype(BF16).reshape(2, rim, wide)
        swap_start(send2, recv2, s2, r2, chunk)
        held.append((y_own, y_rim))

    again = []
    for chunk, (low, high) in enumerate(chunks):
        wide = high - low
        y_own, y_rim = held[chunk]
        v32 = v_ref[:, low:high].astype(F32)
        rims = ghost[:, :, low:high].reshape(2 * rim, wide).astype(F32)
        swap_wait(send2, recv2, s2, r2, chunk)
        y_own = y_own + dot(pick, recv2[:, 0, :, low:high].reshape(2 * rim, wide))
        y_rim = y_rim + recv2[:, 1, :, low:high].reshape(2 * rim, wide).astype(F32)
        first = ((y_own - SHIFT * v32) * INV_HALF).astype(BF16)
        first_rim = ((y_rim - SHIFT * rims) * INV_HALF).reshape(2, rim, wide)
        first_rim = jnp.concatenate(
            [jnp.where(present[side], first_rim[side], 0.0) for side in (0, 1)], axis=0
        ).astype(BF16)
        out_rim = apply(nodes, slots, first, first_rim)
        send3[:, :, low:high] = out_rim.astype(BF16).reshape(2, rim, wide)
        swap_start(send3, recv3, s3, r3, chunk)
        again.append((apply(0, nodes, first, first_rim), first))

    def share(chunk, step, arriving=False):
        low, high = chunks[chunk]
        landing = step - 1 if arriving else bands - 1 - step
        return pltpu.make_async_remote_copy(
            src_ref=filt_ref.at[:, low:high],
            dst_ref=everyone.at[landing, :, low:high],
            send_sem=s4.at[chunk, step],
            recv_sem=r4.at[chunk, landing],
            device_id={"dom": dom, "band": lax.rem(band + step, bands)},
            device_id_type=MESH,
        )

    for chunk, (low, high) in enumerate(chunks):
        wide = high - low
        second, first = again[chunk]
        v32 = v_ref[:, low:high].astype(F32)
        swap_wait(send3, recv3, s3, r3, chunk)
        second = second + dot(pick, recv3[:, :, low:high].reshape(2 * rim, wide))
        filt_ref[:, low:high] = (
            2.0 * (second - SHIFT * first.astype(F32)) * INV_HALF - v32
        ).astype(BF16)
        for step in range(1, bands):
            share(chunk, step).start()

    def place(step):
        return pl.ds(pl.multiple_of(lax.rem(band + step, bands) * cols, 128), cols)

    for step in range(bands):
        if step == 0:
            other = filt_ref[...]
        else:
            for chunk in numbers:
                share(chunk, step, True).wait_recv()
            other = everyone[step - 1]
        product = dot_tn(filt_ref[...], other)
        margin_ref[0, :, place(step)] = product
    for chunk in numbers:
        for step in range(1, bands):
            share(chunk, step).wait_send()


def put_out(filt_ref, margin_ref, filt_hbm, margin_hbm, sem):
    copies = [
        pltpu.make_async_copy(source, target, sem.at[number])
        for number, (source, target) in enumerate(
            ((filt_ref, filt_hbm), (margin_ref, margin_hbm))
        )
    ]
    for copy in copies:
        copy.start()
    for copy in copies:
        copy.wait()


def solution(mesh):
    doms, bands = mesh.shape["dom"], mesh.shape["band"]

    def on_device(vectors, cell_ham, cell_type, cell_nodes, shared_nodes):
        nodes, cols = vectors.shape
        rim = shared_nodes.shape[1] // 2
        slots = nodes + 2 * rim
        rows = cols // doms
        scatter_here = cols % doms == 0 and rows % 8 == 0 and doms == GROUP * GROUP and bands == 2
        inverse_count = 1.0 / (nodes * doms)
        chunks = []
        for width in WIDTHS + (cols,):
            low = chunks[-1][1] if chunks else 0
            if low < cols:
                chunks.append((low, min(low + width, cols)))
        kept = []
        if scatter_here:
            for _, low, high, _ in PIECES:
                wide = high - low
                kept += [
                    pltpu.VMEM((GROUP, GROUP * rows, wide), BF16),
                    pltpu.VMEM((GROUP - 1, GROUP * rows, wide), BF16),
                ]
                kept += [pltpu.SemaphoreType.DMA((2 * (GROUP - 1),))] * 2
                kept += [
                    pltpu.VMEM((GROUP, rows, wide), BF16),
                    pltpu.VMEM((GROUP, rows, wide), F32),
                    pltpu.VMEM((GROUP - 1, rows, wide), BF16),
                ]
                kept += [pltpu.SemaphoreType.DMA((GROUP - 1,))] * 2
        operands = [
            pltpu.with_memory_space_constraint(operand, pltpu.HBM)
            for operand in (cell_type, cell_nodes, shared_nodes, vectors, cell_ham)
        ]
        if scatter_here:
            filtered, margin = pl.pallas_call(
                functools.partial(kernel, doms, bands, tuple(chunks), inverse_count),
                out_shape=(
                    jax.ShapeDtypeStruct((nodes, cols), BF16),
                    jax.ShapeDtypeStruct((1, rows, bands * cols), F32),
                ),
                in_specs=[pl.BlockSpec(memory_space=pltpu.HBM)] * 5,
                out_specs=(pl.BlockSpec(memory_space=pltpu.VMEM),) * 2,
                scratch_shapes=[
                    pltpu.SMEM(cell_type.shape, jnp.int32),
                    pltpu.VMEM(cell_nodes.shape, jnp.int32),
                    pltpu.VMEM(shared_nodes.shape, jnp.int32),
                    pltpu.VMEM(vectors.shape, BF16),
                    pltpu.VMEM(cell_ham.shape, BF16),
                    pltpu.VMEM((cell_nodes.shape[0], slots, slots), BF16),
                    pltpu.VMEM((nodes, nodes), BF16),
                    pltpu.VMEM((nodes, cols), BF16),
                    pltpu.VMEM((slots, cols), F32),
                    pltpu.VMEM((nodes, cols), BF16),
                    pltpu.VMEM((nodes, cols), BF16),
                    pltpu.VMEM((bands, cols, cols), F32),
                    pltpu.VMEM((2, rim, cols), BF16),
                    pltpu.VMEM((2, rim, cols), BF16),
                    pltpu.VMEM((2, 2, rim, cols), BF16),
                    pltpu.VMEM((2, 2, rim, cols), BF16),
                    pltpu.VMEM((2, rim, cols), BF16),
                    pltpu.VMEM((2, rim, cols), BF16),
                    pltpu.VMEM((nodes, cols), BF16),
                ]
                + [pltpu.SemaphoreType.DMA((5,))]
                + [pltpu.SemaphoreType.DMA((len(chunks), 2))] * 6
                + [pltpu.SemaphoreType.DMA((len(chunks) + 1,))] * 2
                + [pltpu.SemaphoreType.REGULAR((2, 2))]
                + kept,
                compiler_params=pltpu.CompilerParams(
                    collective_id=0, has_side_effects=True, vmem_limit_bytes=48 << 20
                ),
            )(*operands)
            filtered, margin = [
                pltpu.with_memory_space_constraint(result, pltpu.VMEM)
                for result in (filtered, margin)
            ]
            filtered, margin = pl.pallas_call(
                put_out,
                out_shape=(
                    jax.ShapeDtypeStruct(filtered.shape, BF16),
                    jax.ShapeDtypeStruct(margin.shape, F32),
                ),
                in_specs=[pl.BlockSpec(memory_space=pltpu.VMEM)] * 2,
                out_specs=(pl.BlockSpec(memory_space=pltpu.HBM),) * 2,
                scratch_shapes=[pltpu.SemaphoreType.DMA((2,))],
            )(filtered, margin)
        else:
            filtered, margin = pl.pallas_call(
                functools.partial(plain_kernel, doms, bands, tuple(chunks)),
                out_shape=(
                    jax.ShapeDtypeStruct((nodes, cols), BF16),
                    jax.ShapeDtypeStruct((1, cols, bands * cols), F32),
                ),
                in_specs=[pl.BlockSpec(memory_space=pltpu.HBM)] * 5,
                out_specs=(pl.BlockSpec(memory_space=pltpu.VMEM),) * 2,
                scratch_shapes=[
                    pltpu.SMEM(cell_type.shape, jnp.int32),
                    pltpu.VMEM(cell_nodes.shape, jnp.int32),
                    pltpu.VMEM(shared_nodes.shape, jnp.int32),
                    pltpu.VMEM(vectors.shape, BF16),
                    pltpu.VMEM(cell_ham.shape, BF16),
                    pltpu.VMEM((cell_nodes.shape[0], slots, slots), BF16),
                    pltpu.VMEM((2, rim, cols), BF16),
                    pltpu.VMEM((2, rim, cols), BF16),
                    pltpu.VMEM((2, 2, rim, cols), BF16),
                    pltpu.VMEM((2, 2, rim, cols), BF16),
                    pltpu.VMEM((2, rim, cols), BF16),
                    pltpu.VMEM((2, rim, cols), BF16),
                    pltpu.VMEM((max(bands - 1, 1), nodes, cols), BF16),
                ]
                + [pltpu.SemaphoreType.DMA((5,))]
                + [pltpu.SemaphoreType.DMA((len(chunks), 2))] * 6
                + [pltpu.SemaphoreType.DMA((len(chunks), bands))] * 2,
                compiler_params=pltpu.CompilerParams(
                    collective_id=0, has_side_effects=True, vmem_limit_bytes=48 << 20
                ),
            )(*operands)
            margin = inverse_count * lax.psum_scatter(
                margin, "dom", scatter_dimension=1, tiled=True
            )
        return filtered, margin

    in_specs = (P("dom", "band"), P(), P("dom"), P("dom", None), P("dom", None))
    out_specs = (P("dom", "band"), P("band", "dom", None))
    return jax.shard_map(
        on_device, mesh=mesh, in_specs=in_specs, out_specs=out_specs, check_vma=False
    )
```

```python
import functools

import jax
import jax.numpy as jnp
from jax import lax
from jax.experimental import pallas as pl
from jax.experimental.pallas import tpu as pltpu
from jax.sharding import PartitionSpec as P

SHIFT = 0.5
INV_HALF = 0.5
GROUP = 4
WIDTHS = (128, 128, 128)
PIECES = ((0, 0, 256, 0), (0, 256, 384, 1), (1, 0, 256, 0), (1, 256, 384, 1))
ORDER = (0, 2, 1, 3)
MESH = pl.DeviceIdType.MESH
F32 = jnp.float32
BF16 = jnp.bfloat16


def dot(a, b):
    return jnp.dot(a, b, preferred_element_type=F32)


def dot_tn(a, b):
    return lax.dot_general(a, b, (((0,), (0,)), ((), ())), preferred_element_type=F32)


def dot_nt(a, b):
    return lax.dot_general(a, b, (((1,), (1,)), ((), ())), preferred_element_type=F32)


def one_hot(rows, index_row):
    spots = lax.broadcasted_iota(jnp.int32, (rows, index_row.shape[1]), 0)
    return jnp.where(spots == index_row, 1.0, 0.0).astype(BF16)


def kernel(
    doms, bands, chunks, inverse_count,
    type_hbm, nodes_hbm, shared_hbm, v_hbm, ham_hbm,
    filt_ref, margin_ref,
    type_ref, nodes_ref, shared_ref, v_ref, ham, hp,
    perm, v_own, base, first_ref, filt, product_ref,
    send1, ghost, send2, recv2, send3, recv3, everyone,
    in_sem, s1, r1, s2, r2, s3, r3, s4, r4, known,
    *held_refs,
):
    dom = lax.axis_index("dom")
    band = lax.axis_index("band")
    nodes, cols = v_ref.shape
    cells = nodes_ref.shape[0]
    rim = shared_ref.shape[1] // 2
    edge = 2 * rim
    slots = nodes + edge
    present = (dom > 0, dom < doms - 1)
    beside = (jnp.maximum(dom - 1, 0), jnp.minimum(dom + 1, doms - 1))

    load_shared, load_v, load_nodes, load_type, load_ham = [
        pltpu.make_async_copy(source, target, in_sem.at[number])
        for number, (source, target) in enumerate(
            (
                (shared_hbm, shared_ref),
                (v_hbm, v_ref),
                (nodes_hbm, nodes_ref),
                (type_hbm, type_ref),
                (ham_hbm, ham),
            )
        )
    ]

    for load in (load_shared, load_v, load_nodes, load_type, load_ham):
        load.start()
    barrier = pltpu.get_barrier_semaphore()

    def greet(other_dom, other_band):
        pl.semaphore_signal(
            barrier, inc=1,
            device_id={"dom": other_dom, "band": other_band},
            device_id_type=MESH,
        )

    for side in (0, 1):
        @pl.when(present[side])
        def _():
            greet(beside[side], band)
    for step in range(1, bands):
        greet(dom, lax.rem(band + step, bands))

    for side in (0, 1):
        @pl.when(jnp.logical_not(present[side]))
        def _():
            ghost[side] = jnp.zeros((rim, cols), BF16)
            recv2[side] = jnp.zeros((2, rim, cols), BF16)
            recv3[side] = jnp.zeros((rim, cols), BF16)

    far = lax.rem(dom, 2)
    in_order = ((far, dom + 2 * far - 1), (1 - far, dom + 1 - 2 * far))

    def swap(source, target, sent, got, chunk, side, other, arriving):
        low, high = chunks[chunk]
        landing = side if arriving else 1 - side
        return pltpu.make_async_remote_copy(
            src_ref=source.at[side, ..., low:high],
            dst_ref=target.at[landing, ..., low:high],
            send_sem=sent.at[chunk, side],
            recv_sem=got.at[chunk, landing],
            device_id={"dom": other, "band": band},
            device_id_type=MESH,
        )

    def swap_start(*args):
        for side, other in in_order:
            @pl.when(jnp.logical_and(other >= 0, other < doms))
            def _():
                swap(*args, side, other, False).start()

    def swap_wait(*args):
        for side in (0, 1):
            @pl.when(present[side])
            def _():
                swap(*args, side, beside[side], True).wait()

    load_shared.wait()
    load_v.wait()
    pick = one_hot(nodes, shared_ref[...])
    send1[...] = dot_tn(pick, v_ref[...]).astype(BF16).reshape(2, rim, cols)

    pl.semaphore_wait(
        barrier,
        bands - 1 + jnp.where(present[0], 1, 0) + jnp.where(present[1], 1, 0),
    )
    numbers = range(len(chunks))
    for chunk in numbers:
        swap_start(send1, ghost, s1, r1, chunk)

    free = 1.0 - jnp.sum(pick.astype(F32), axis=1, keepdims=True)
    below = lax.broadcasted_iota(jnp.int32, (nodes, nodes), 0) > lax.broadcasted_iota(
        jnp.int32, (nodes, nodes), 1
    )
    rank = dot(
        jnp.where(below, 1.0, 0.0).astype(BF16),
        jnp.broadcast_to(free, (nodes, 128)).astype(BF16),
    )[:, :1]
    spots = lax.broadcasted_iota(jnp.int32, (nodes, nodes - edge), 1).astype(F32)
    rest = jnp.where(jnp.logical_and(spots == rank, free > 0.5), 1.0, 0.0).astype(BF16)
    perm[:, :edge] = pick
    perm[:, edge:] = rest
    count = lax.broadcasted_iota(jnp.int32, (nodes, 128), 0)
    digits = jnp.where(
        lax.broadcasted_iota(jnp.int32, (nodes, 128), 1) == 0, count // 32, count % 32
    )
    digits = dot_tn(perm[...], digits.astype(BF16))
    name = (32.0 * digits[:, :1] + digits[:, 1:2]).astype(jnp.int32)
    v_own[:edge] = send1[...].reshape(edge, cols)
    v_own[edge:] = dot_tn(rest, v_ref[...]).astype(BF16)

    load_nodes.wait()
    load_type.wait()
    load_ham.wait()
    spreads = []
    for cell in range(cells):
        slot = nodes_ref[cell : cell + 1, :]
        slot = jnp.where(slot < rim, slot + nodes, jnp.where(slot < nodes + rim, slot - rim, slot))
        outside = lax.broadcasted_iota(jnp.int32, (edge, slot.shape[1]), 0) + nodes
        spreads.append([
            jnp.where(rows == slot, 1.0, 0.0).astype(BF16)
            for rows in (name[:edge], name[edge:], outside)
        ])

    def assemble(rows, part):
        for cell in range(cells):
            wanted = dot(spreads[cell][part], ham[type_ref[cell]]).astype(BF16)
            hp[cell, rows[0] : rows[1]] = dot_nt(
                wanted, jnp.concatenate(spreads[cell], axis=0)
            ).astype(BF16)

    def apply(rows, columns, field):
        total = dot(hp[0, rows[0] : rows[1], columns[0] : columns[1]], field)
        for cell in range(1, cells):
            total += dot(hp[cell, rows[0] : rows[1], columns[0] : columns[1]], field)
        return total

    on_edge, inner, owned, outer = (0, edge), (edge, nodes), (0, nodes), (nodes, slots)
    assemble(outer, 2)
    base[nodes:] = apply(outer, owned, v_own[...])
    assemble(on_edge, 0)
    base[:edge] = apply(on_edge, owned, v_own[...])

    held = []
    for chunk, (low, high) in enumerate(chunks):
        wide = high - low
        swap_wait(send1, ghost, s1, r1, chunk)
        rims = ghost[:, :, low:high].reshape(edge, wide)
        y_rim = base[nodes:, low:high] + apply(outer, outer, rims)
        send2[:, 0, :, low:high] = y_rim.astype(BF16).reshape(2, rim, wide)
        y_edge = base[:edge, low:high] + apply(on_edge, outer, rims)
        send2[:, 1, :, low:high] = y_edge.astype(BF16).reshape(2, rim, wide)
        swap_start(send2, recv2, s2, r2, chunk)
        held.append((y_edge, y_rim))
    assemble(inner, 1)
    y_inner = apply(inner, owned, v_own[...]) + apply(inner, outer, ghost[...].reshape(edge, cols))
    first_ref[edge:] = ((y_inner - SHIFT * v_own[edge:].astype(F32)) * INV_HALF).astype(BF16)
    base[...] = apply((0, slots), inner, first_ref[edge:, :])

    def finish(second, first, v):
        return (2.0 * (second - SHIFT * first.astype(F32)) * INV_HALF - v.astype(F32)).astype(BF16)

    again = []
    for chunk, (low, high) in enumerate(chunks):
        wide = high - low
        y_edge, y_rim = held[chunk]
        v32 = v_own[:edge, low:high].astype(F32)
        rims = ghost[:, :, low:high].reshape(edge, wide).astype(F32)
        swap_wait(send2, recv2, s2, r2, chunk)
        y_edge = y_edge + recv2[:, 0, :, low:high].reshape(edge, wide).astype(F32)
        y_rim = y_rim + recv2[:, 1, :, low:high].reshape(edge, wide).astype(F32)
        first = ((y_edge - SHIFT * v32) * INV_HALF).astype(BF16)
        first_rim = ((y_rim - SHIFT * rims) * INV_HALF).reshape(2, rim, wide)
        first_rim = jnp.concatenate(
            [jnp.where(present[side], first_rim[side], 0.0) for side in (0, 1)], axis=0
        ).astype(BF16)
        out_rim = base[nodes:, low:high] + apply(outer, on_edge, first) + apply(outer, outer, first_rim)
        send3[:, :, low:high] = out_rim.astype(BF16).reshape(2, rim, wide)
        swap_start(send3, recv3, s3, r3, chunk)
        out = base[:nodes, low:high] + apply(owned, on_edge, first) + apply(owned, outer, first_rim)
        filt[edge:, low:high] = finish(
            out[edge:], first_ref[edge:, low:high], v_own[edge:, low:high]
        )
        again.append((out[:edge], first))

    inside, stack = lax.rem(dom, GROUP), dom // GROUP
    linked = (stack > 0, stack < doms // GROUP - 1)

    def announce(turn):
        if turn:
            hear(turn - 1)
        for side in (0, 1):
            @pl.when(linked[side])
            def _():
                pl.semaphore_signal(
                    known.at[turn, 1 - side], inc=1,
                    device_id={"dom": dom + (GROUP if side else -GROUP), "band": band},
                    device_id_type=MESH,
                )

    def hear(turn):
        for side in (0, 1):
            @pl.when(linked[side])
            def _():
                pl.semaphore_wait(known.at[turn, side], 1)

    def share(part):
        rows, (low, high) = ((edge, nodes), (0, cols)) if part == 0 else ((0, edge), chunks[part - 1])
        return pltpu.make_async_remote_copy(
            src_ref=filt.at[rows[0] : rows[1], low:high],
            dst_ref=everyone.at[rows[0] : rows[1], low:high],
            send_sem=s4.at[part],
            recv_sem=r4.at[part],
            device_id={"dom": dom, "band": 1 - band},
            device_id_type=MESH,
        )

    share(0).start()
    product_ref[0] = dot_tn(filt[edge:], filt[edge:])
    share(0).wait_recv()
    product_ref[1] = dot_tn(filt[edge:], everyone[edge:])
    def place(step, low, high):
        start = lax.rem(band + step, bands) * cols + low
        return pl.ds(pl.multiple_of(start, 128), high - low)

    def others(step):
        if step == 0:
            return filt[:edge]
        for chunk in numbers[2:]:
            share(chunk + 1).wait_recv()
        return everyone[:edge]

    rows = cols // doms
    where = (inside, stack)

    def device(axis, index):
        return stack * GROUP + index if axis == 0 else index * GROUP + inside

    def pass_on(axis, source, target, sent, got, away, arriving=False, half=None):
        other = lax.rem(where[axis] + away, GROUP)
        landing = away - 1 if arriving else GROUP - 1 - away
        cut, shift = 2 * rows, (GROUP - 1 if half else 0)
        return pltpu.make_async_remote_copy(
            src_ref=source.at[other] if half is None else source.at[other, half * cut : (half + 1) * cut],
            dst_ref=target.at[landing] if half is None else target.at[landing, half * cut : (half + 1) * cut],
            send_sem=sent.at[away - 1 + shift],
            recv_sem=got.at[landing + shift],
            device_id={"dom": device(axis, other), "band": band},
            device_id_type=MESH,
        )

    def leave(axis, *args, half=None):
        mine = where[axis]
        if axis == 0:
            targets = [
                mine + (1 - 2 * lax.rem(mine, 2)) * x + (2 - 4 * (mine // 2)) * y
                for x, y in ((1, 1), (1, 0), (0, 1))
            ]
        else:
            upper = mine // 2
            targets = [3 - 3 * upper, 2 - upper, mine + 1 - 2 * lax.rem(mine, 2)]
        for target in targets:
            pass_on(axis, *args, lax.rem(target - mine + GROUP, GROUP), half=half).start()

    def own_rows(step, low, high, axis):
        if axis:
            start = pl.multiple_of(stack * (GROUP * rows), 8)
            return product_ref[step, pl.ds(start, GROUP * rows), low:high]
        starts = [pl.multiple_of((layer * GROUP + inside) * rows, 8) for layer in range(GROUP)]
        return jnp.concatenate(
            [product_ref[step, pl.ds(start, rows), low:high] for start in starts], axis=0
        )

    away_range = range(1, GROUP)
    works = [held_refs[number : number + 9] for number in range(0, len(held_refs), 9)]
    ready = chunks[1][1]
    ahead = GROUP * rows * 2

    def early(step):
        other = filt if step == 0 else everyone
        product = product_ref[step, :ahead, :ready] + dot_tn(filt[:edge, :ahead], other[:edge, :ready])
        for (its_step, low, high, axis), work in zip(PIECES, works):
            if its_step == step and axis == 0 and high <= ready:
                part, arrived, s5, r5 = work[:4]
                for member in range(GROUP):
                    part[member, : 2 * rows] = jnp.concatenate(
                        [
                            product[(layer * GROUP + member) * rows : (layer * GROUP + member + 1) * rows, low:high]
                            for layer in range(2)
                        ],
                        axis=0,
                    ).astype(BF16)
                leave(axis, part, arrived, s5, r5, half=0)

    for chunk, (low, high) in enumerate(chunks):
        wide = high - low
        second, first = again[chunk]
        swap_wait(send3, recv3, s3, r3, chunk)
        if chunk < 2:
            announce(chunk)
        second = second + recv3[:, :, low:high].reshape(edge, wide).astype(F32)
        filt[:edge, low:high] = finish(second, first, v_own[:edge, low:high])
        share(chunk + 1).start()
        if chunk == 1:
            early(0)
    for step in range(bands):
        product = product_ref[step] + dot_tn(filt[:edge], others(step))
        product_ref[step] = product
        for (its_step, low, high, axis), work in zip(PIECES, works):
            if its_step != step:
                continue
            part, arrived, s5, r5 = work[:4]
            split = axis == 0 and high <= ready
            for member in range(GROUP):
                if axis == 0:
                    block = jnp.concatenate(
                        [
                            product[(layer * GROUP + member) * rows : (layer * GROUP + member + 1) * rows, low:high]
                            for layer in range(GROUP)
                        ],
                        axis=0,
                    )
                else:
                    block = product[member * GROUP * rows : (member + 1) * GROUP * rows, low:high]
                if split:
                    part[member, 2 * rows :] = block[2 * rows :].astype(BF16)
                else:
                    part[member] = block.astype(BF16)
            if (step, axis) == (0, 1):
                hear(1)
            leave(axis, part, arrived, s5, r5, half=1 if split else None)
        if step == 0:
            for chunk in (0, 1):
                share(chunk + 1).wait_recv()
            early(1)
    filt_ref[...] = dot(perm[...], filt[...]).astype(BF16)
    for number in ORDER:
        step, low, high, axis = PIECES[number]
        part, arrived, s5, r5, part2, own_part2, arrived2, s6, r6 = works[number]
        total = own_rows(step, low, high, axis)
        for away in away_range:
            for half in (0, 1) if axis == 0 and high <= ready else (None,):
                pass_on(axis, part, arrived, s5, r5, away, True, half).wait_recv()
            total += arrived[away - 1].astype(F32)
        for layer in range(GROUP):
            block = total[layer * rows : (layer + 1) * rows]
            own_part2[layer] = block
            part2[layer] = block.astype(BF16)
        leave(1 - axis, part2, arrived2, s6, r6)
    for number in ORDER:
        step, low, high, axis = PIECES[number]
        part, arrived, s5, r5, part2, own_part2, arrived2, s6, r6 = works[number]
        total = own_part2[where[1 - axis]]
        for away in away_range:
            pass_on(1 - axis, part2, arrived2, s6, r6, away, True).wait_recv()
            total += arrived2[away - 1].astype(F32)
        margin_ref[0, :, place(step, low, high)] = total * inverse_count
    for number, (step, low, high, axis) in enumerate(PIECES):
        part, arrived, s5, r5, part2, own_part2, arrived2, s6, r6 = works[number]
        for away in away_range:
            for half in (0, 1) if axis == 0 and high <= ready else (None,):
                pass_on(axis, part, arrived, s5, r5, away, False, half).wait_send()
            pass_on(1 - axis, part2, arrived2, s6, r6, away).wait_send()
    for part in range(len(chunks) + 1):
        share(part).wait_send()


def plain_kernel(
    doms, bands, chunks,
    type_hbm, nodes_hbm, shared_hbm, v_hbm, ham_hbm,
    filt_ref, margin_ref,
    type_ref, nodes_ref, shared_ref, v_ref, ham, hp,
    send1, ghost, send2, recv2, send3, recv3, everyone,
    in_sem, s1, r1, s2, r2, s3, r3, s4, r4,
):
    dom = lax.axis_index("dom")
    band = lax.axis_index("band")
    nodes, cols = v_ref.shape
    cells = nodes_ref.shape[0]
    rim = shared_ref.shape[1] // 2
    slots = nodes + 2 * rim
    present = (dom > 0, dom < doms - 1)
    beside = (jnp.maximum(dom - 1, 0), jnp.minimum(dom + 1, doms - 1))

    load_shared, load_v, load_nodes, load_type, load_ham = [
        pltpu.make_async_copy(source, target, in_sem.at[number])
        for number, (source, target) in enumerate(
            (
                (shared_hbm, shared_ref),
                (v_hbm, v_ref),
                (nodes_hbm, nodes_ref),
                (type_hbm, type_ref),
                (ham_hbm, ham),
            )
        )
    ]

    barrier = pltpu.get_barrier_semaphore()

    def greet(other_dom, other_band):
        pl.semaphore_signal(
            barrier, inc=1,
            device_id={"dom": other_dom, "band": other_band},
            device_id_type=MESH,
        )

    for side in (0, 1):
        @pl.when(present[side])
        def _():
            greet(beside[side], band)
    for step in range(1, bands):
        greet(dom, lax.rem(band + step, bands))
    for load in (load_shared, load_v, load_nodes, load_type, load_ham):
        load.start()

    for side in (0, 1):
        @pl.when(jnp.logical_not(present[side]))
        def _():
            ghost[side] = jnp.zeros((rim, cols), BF16)
            recv2[side] = jnp.zeros((2, rim, cols), BF16)
            recv3[side] = jnp.zeros((rim, cols), BF16)

    def swap(source, target, sent, got, chunk, side, arriving):
        low, high = chunks[chunk]
        landing = side if arriving else 1 - side
        return pltpu.make_async_remote_copy(
            src_ref=source.at[side, ..., low:high],
            dst_ref=target.at[landing, ..., low:high],
            send_sem=sent.at[chunk, side],
            recv_sem=got.at[chunk, landing],
            device_id={"dom": beside[side], "band": band},
            device_id_type=MESH,
        )

    def swap_start(*args):
        for side in (0, 1):
            @pl.when(present[side])
            def _():
                swap(*args, side, False).start()

    def swap_wait(*args):
        for side in (0, 1):
            @pl.when(present[side])
            def _():
                swap(*args, side, True).wait()

    load_shared.wait()
    load_v.wait()
    pick = one_hot(nodes, shared_ref[...])
    send1[...] = dot_tn(pick, v_ref[...]).astype(BF16).reshape(2, rim, cols)

    pl.semaphore_wait(
        barrier,
        bands - 1 + jnp.where(present[0], 1, 0) + jnp.where(present[1], 1, 0),
    )
    numbers = range(len(chunks))
    for chunk in numbers:
        swap_start(send1, ghost, s1, r1, chunk)

    load_nodes.wait()
    load_type.wait()
    load_ham.wait()
    for cell in range(cells):
        slot = nodes_ref[cell : cell + 1, :]
        slot = jnp.where(slot < rim, slot + nodes, jnp.where(slot < nodes + rim, slot - rim, slot))
        spread = one_hot(slots, slot)
        spread_ham = dot(spread, ham[type_ref[cell]]).astype(BF16)
        hp[cell] = dot_nt(spread_ham, spread).astype(BF16)

    def apply(low, high, own, rims):
        total = dot(hp[0, low:high, :nodes], own) + dot(hp[0, low:high, nodes:], rims)
        for cell in range(1, cells):
            total += dot(hp[cell, low:high, :nodes], own) + dot(hp[cell, low:high, nodes:], rims)
        return total

    held = []
    for chunk, (low, high) in enumerate(chunks):
        wide = high - low
        swap_wait(send1, ghost, s1, r1, chunk)
        v = v_ref[:, low:high]
        rims = ghost[:, :, low:high].reshape(2 * rim, wide)
        y_own = apply(0, nodes, v, rims)
        send2[:, 1, :, low:high] = (
            dot_tn(pick, y_own.astype(BF16)).astype(BF16).reshape(2, rim, wide)
        )
        y_rim = apply(nodes, slots, v, rims)
        send2[:, 0, :, low:high] = y_rim.astype(BF16).reshape(2, rim, wide)
        swap_start(send2, recv2, s2, r2, chunk)
        held.append((y_own, y_rim))

    again = []
    for chunk, (low, high) in enumerate(chunks):
        wide = high - low
        y_own, y_rim = held[chunk]
        v32 = v_ref[:, low:high].astype(F32)
        rims = ghost[:, :, low:high].reshape(2 * rim, wide).astype(F32)
        swap_wait(send2, recv2, s2, r2, chunk)
        y_own = y_own + dot(pick, recv2[:, 0, :, low:high].reshape(2 * rim, wide))
        y_rim = y_rim + recv2[:, 1, :, low:high].reshape(2 * rim, wide).astype(F32)
        first = ((y_own - SHIFT * v32) * INV_HALF).astype(BF16)
        first_rim = ((y_rim - SHIFT * rims) * INV_HALF).reshape(2, rim, wide)
        first_rim = jnp.concatenate(
            [jnp.where(present[side], first_rim[side], 0.0) for side in (0, 1)], axis=0
        ).astype(BF16)
        out_rim = apply(nodes, slots, first, first_rim)
        send3[:, :, low:high] = out_rim.astype(BF16).reshape(2, rim, wide)
        swap_start(send3, recv3, s3, r3, chunk)
        again.append((apply(0, nodes, first, first_rim), first))

    def share(chunk, step, arriving=False):
        low, high = chunks[chunk]
        landing = step - 1 if arriving else bands - 1 - step
        return pltpu.make_async_remote_copy(
            src_ref=filt_ref.at[:, low:high],
            dst_ref=everyone.at[landing, :, low:high],
            send_sem=s4.at[chunk, step],
            recv_sem=r4.at[chunk, landing],
            device_id={"dom": dom, "band": lax.rem(band + step, bands)},
            device_id_type=MESH,
        )

    for chunk, (low, high) in enumerate(chunks):
        wide = high - low
        second, first = again[chunk]
        v32 = v_ref[:, low:high].astype(F32)
        swap_wait(send3, recv3, s3, r3, chunk)
        second = second + dot(pick, recv3[:, :, low:high].reshape(2 * rim, wide))
        filt_ref[:, low:high] = (
            2.0 * (second - SHIFT * first.astype(F32)) * INV_HALF - v32
        ).astype(BF16)
        for step in range(1, bands):
            share(chunk, step).start()

    def place(step):
        return pl.ds(pl.multiple_of(lax.rem(band + step, bands) * cols, 128), cols)

    for step in range(bands):
        if step == 0:
            other = filt_ref[...]
        else:
            for chunk in numbers:
                share(chunk, step, True).wait_recv()
            other = everyone[step - 1]
        product = dot_tn(filt_ref[...], other)
        margin_ref[0, :, place(step)] = product
    for chunk in numbers:
        for step in range(1, bands):
            share(chunk, step).wait_send()


def put_out(filt_ref, margin_ref, filt_hbm, margin_hbm, sem):
    copies = [
        pltpu.make_async_copy(source, target, sem.at[number])
        for number, (source, target) in enumerate(
            ((filt_ref, filt_hbm), (margin_ref, margin_hbm))
        )
    ]
    for copy in copies:
        copy.start()
    for copy in copies:
        copy.wait()


def solution(mesh):
    doms, bands = mesh.shape["dom"], mesh.shape["band"]

    def on_device(vectors, cell_ham, cell_type, cell_nodes, shared_nodes):
        nodes, cols = vectors.shape
        rim = shared_nodes.shape[1] // 2
        slots = nodes + 2 * rim
        rows = cols // doms
        scatter_here = cols % doms == 0 and rows % 8 == 0 and doms == GROUP * GROUP and bands == 2
        inverse_count = 1.0 / (nodes * doms)
        chunks = []
        for width in WIDTHS + (cols,):
            low = chunks[-1][1] if chunks else 0
            if low < cols:
                chunks.append((low, min(low + width, cols)))
        kept = []
        if scatter_here:
            for _, low, high, _ in PIECES:
                wide = high - low
                kept += [
                    pltpu.VMEM((GROUP, GROUP * rows, wide), BF16),
                    pltpu.VMEM((GROUP - 1, GROUP * rows, wide), BF16),
                ]
                kept += [pltpu.SemaphoreType.DMA((2 * (GROUP - 1),))] * 2
                kept += [
                    pltpu.VMEM((GROUP, rows, wide), BF16),
                    pltpu.VMEM((GROUP, rows, wide), F32),
                    pltpu.VMEM((GROUP - 1, rows, wide), BF16),
                ]
                kept += [pltpu.SemaphoreType.DMA((GROUP - 1,))] * 2
        operands = [
            pltpu.with_memory_space_constraint(operand, pltpu.HBM)
            for operand in (cell_type, cell_nodes, shared_nodes, vectors, cell_ham)
        ]
        if scatter_here:
            filtered, margin = pl.pallas_call(
                functools.partial(kernel, doms, bands, tuple(chunks), inverse_count),
                out_shape=(
                    jax.ShapeDtypeStruct((nodes, cols), BF16),
                    jax.ShapeDtypeStruct((1, rows, bands * cols), F32),
                ),
                in_specs=[pl.BlockSpec(memory_space=pltpu.HBM)] * 5,
                out_specs=(pl.BlockSpec(memory_space=pltpu.VMEM),) * 2,
                scratch_shapes=[
                    pltpu.SMEM(cell_type.shape, jnp.int32),
                    pltpu.VMEM(cell_nodes.shape, jnp.int32),
                    pltpu.VMEM(shared_nodes.shape, jnp.int32),
                    pltpu.VMEM(vectors.shape, BF16),
                    pltpu.VMEM(cell_ham.shape, BF16),
                    pltpu.VMEM((cell_nodes.shape[0], slots, slots), BF16),
                    pltpu.VMEM((nodes, nodes), BF16),
                    pltpu.VMEM((nodes, cols), BF16),
                    pltpu.VMEM((slots, cols), F32),
                    pltpu.VMEM((nodes, cols), BF16),
                    pltpu.VMEM((nodes, cols), BF16),
                    pltpu.VMEM((bands, cols, cols), F32),
                    pltpu.VMEM((2, rim, cols), BF16),
                    pltpu.VMEM((2, rim, cols), BF16),
                    pltpu.VMEM((2, 2, rim, cols), BF16),
                    pltpu.VMEM((2, 2, rim, cols), BF16),
                    pltpu.VMEM((2, rim, cols), BF16),
                    pltpu.VMEM((2, rim, cols), BF16),
                    pltpu.VMEM((nodes, cols), BF16),
                ]
                + [pltpu.SemaphoreType.DMA((5,))]
                + [pltpu.SemaphoreType.DMA((len(chunks), 2))] * 6
                + [pltpu.SemaphoreType.DMA((len(chunks) + 1,))] * 2
                + [pltpu.SemaphoreType.REGULAR((2, 2))]
                + kept,
                compiler_params=pltpu.CompilerParams(
                    collective_id=0, has_side_effects=True, vmem_limit_bytes=48 << 20
                ),
            )(*operands)
            filtered, margin = [
                pltpu.with_memory_space_constraint(result, pltpu.VMEM)
                for result in (filtered, margin)
            ]
            filtered, margin = pl.pallas_call(
                put_out,
                out_shape=(
                    jax.ShapeDtypeStruct(filtered.shape, BF16),
                    jax.ShapeDtypeStruct(margin.shape, F32),
                ),
                in_specs=[pl.BlockSpec(memory_space=pltpu.VMEM)] * 2,
                out_specs=(pl.BlockSpec(memory_space=pltpu.HBM),) * 2,
                scratch_shapes=[pltpu.SemaphoreType.DMA((2,))],
            )(filtered, margin)
        else:
            filtered, margin = pl.pallas_call(
                functools.partial(plain_kernel, doms, bands, tuple(chunks)),
                out_shape=(
                    jax.ShapeDtypeStruct((nodes, cols), BF16),
                    jax.ShapeDtypeStruct((1, cols, bands * cols), F32),
                ),
                in_specs=[pl.BlockSpec(memory_space=pltpu.HBM)] * 5,
                out_specs=(pl.BlockSpec(memory_space=pltpu.VMEM),) * 2,
                scratch_shapes=[
                    pltpu.SMEM(cell_type.shape, jnp.int32),
                    pltpu.VMEM(cell_nodes.shape, jnp.int32),
                    pltpu.VMEM(shared_nodes.shape, jnp.int32),
                    pltpu.VMEM(vectors.shape, BF16),
                    pltpu.VMEM(cell_ham.shape, BF16),
                    pltpu.VMEM((cell_nodes.shape[0], slots, slots), BF16),
                    pltpu.VMEM((2, rim, cols), BF16),
                    pltpu.VMEM((2, rim, cols), BF16),
                    pltpu.VMEM((2, 2, rim, cols), BF16),
                    pltpu.VMEM((2, 2, rim, cols), BF16),
                    pltpu.VMEM((2, rim, cols), BF16),
                    pltpu.VMEM((2, rim, cols), BF16),
                    pltpu.VMEM((max(bands - 1, 1), nodes, cols), BF16),
                ]
                + [pltpu.SemaphoreType.DMA((5,))]
                + [pltpu.SemaphoreType.DMA((len(chunks), 2))] * 6
                + [pltpu.SemaphoreType.DMA((len(chunks), bands))] * 2,
                compiler_params=pltpu.CompilerParams(
                    collective_id=0, has_side_effects=True, vmem_limit_bytes=48 << 20
                ),
            )(*operands)
            margin = inverse_count * lax.psum_scatter(
                margin, "dom", scatter_dimension=1, tiled=True
            )
        return filtered, margin

    in_specs = (P("dom", "band"), P(), P("dom"), P("dom", None), P("dom", None))
    out_specs = (P("dom", "band"), P("band", "dom", None))
    return jax.shard_map(
        on_device, mesh=mesh, in_specs=in_specs, out_specs=out_specs, check_vma=False
    )
```
